256 devices in a mesh: group: 32 (over z, x_lo, core), rep: 8 (over x_hi, y).
Axes of the slice: x: 4 (x_hi: 2, x_lo: 2; x = x_hi * 2 + x_lo), y: 4, z: 8, core: 2. Of those that a mesh axis runs over, the one named last changes fastest.
Arguments:
- queries: bfloat16 [256, 256, 3072], P(('group', 'rep')), may hold values from -46 to 46
- keys: bfloat16 [256, 256, 3072], P(('group', 'rep')), may hold values from -46 to 46
- values: bfloat16 [256, 256, 3072], P(('group', 'rep')), may hold values from -24 to 24
- grad_output: bfloat16 [256, 256, 3072], P(('group', 'rep')), may hold values from -6 to 6
- weight_codes: bfloat16 [3072, 3072], P('group'), may hold values from -4 to 4
- weight_scales: float32 [3072, 12], P('group'), may hold values from 0.006 to 0.06
Outputs:
- grad_queries: bfloat16 [256, 256, 3072], P(('group', 'rep'))
- grad_keys: bfloat16 [256, 256, 3072], P(('group', 'rep'))
- grad_values: bfloat16 [256, 256, 3072], P(('group', 'rep'))
- grad_weight: float32 [3072, 3072], P(('group', 'rep'))
The draws below stay inside these ranges and needn't reach their ends.
All inputs are finite; a program needn't handle non-finite values.
Results may differ from the reference program's by a relative error of at most 0.029.
Values may be sent and summed in bfloat16 or wider, within the bound.
No kernel may reach another device: no remote copies, remote signals or barrier semaphores. Data moves between devices by JAX's collectives and lax.ppermute only.
A program may use at most 128 MiB of HBM per device.

```python
import math
import jax
import jax.numpy as jnp
from jax import lax

H = 24
HD = 128
E = 3072
BLOCK = 256
SEQ = 256
IMG_DEV = 1
ROWS = 3072
IMAGES = 256
N_GROUP = 32
N_REP = 8


def make_pairs(key):
    base = jax.random.fold_in(key, 7)
    key_query, key_keys = jax.random.split(base, 2)
    shape = (IMAGES, SEQ, H, HD)
    query = jnp.clip(jax.random.normal(key_query, shape, jnp.float32), -4.0, 4.0)
    keyset = jnp.clip(jax.random.normal(key_keys, shape, jnp.float32), -4.0, 4.0)
    query = query.reshape(IMAGES, SEQ, H * HD).astype(jnp.bfloat16)
    keyset = keyset.reshape(IMAGES, SEQ, H * HD).astype(jnp.bfloat16)
    return (query, keyset)


def draw_queries(key, part):
    return make_pairs(key)[0]


def draw_keys(key, part):
    return make_pairs(key)[1]


def with_spikes(result, stream_key, source, target, shards_of, factor):
    owner, partner = [(jnp.arange(result.shape[dim]) // (result.shape[dim] // shards_of)).reshape([-1 if axis == dim else 1 for axis in range(result.ndim)]) for dim in (source, target)]
    chosen = jax.random.permutation(stream_key, shards_of)[partner]
    strong = (owner == chosen) | (owner == (partner + shards_of // 2) % shards_of)
    return jnp.where(strong, factor * result, result)


def block_levels(key, extent, shards, low, top_value):
    loudness, own = 1.0, jax.random.fold_in(key, 6)
    for position, shards_of in shards:
        steps = jnp.exp(jax.random.uniform(jax.random.fold_in(own, position), (shards_of,), jnp.float32, low / len(shards), top_value / len(shards)))
        loudness = loudness * jnp.repeat(steps, extent[position] // shards_of).reshape([-1 if axis == position else 1 for axis in range(len(extent))])
    return loudness


def bell_draw(key, dims, deviation, most, shards=(), kind=jnp.bfloat16):
    loudness = block_levels(key, dims, shards, -0.22, 0.18) if shards else 1.0
    entries = jax.random.normal(key, dims, jnp.float32) * deviation * loudness
    return jnp.minimum(jnp.maximum(entries, -most), most).astype(kind)


def bell_draw_with(key, extent, scale, reach, cuts, heavy, dtype=jnp.bfloat16):
    values = scale * jax.random.normal(key, extent, jnp.float32)
    if cuts:
        values = values * block_levels(key, extent, cuts, -0.22, 0.18)
    return jnp.clip(with_spikes(values, jax.random.fold_in(key, 3), *heavy), -reach, reach).astype(dtype)


def setup_inputs(seed: int = 0) -> dict:
    key_of = jax.random.split(jax.random.key(seed), 7)
    return {
        "queries": draw_queries(jax.random.fold_in(key_of[6], 71), 0),
        "keys": draw_keys(jax.random.fold_in(key_of[6], 71), 0),
        "values": bell_draw_with(key_of[2], (IMAGES, SEQ, ROWS), 1.0, 24.0, ((0, 256),), (0, 2, 256, 6.0)),
        "grad_output": bell_draw(key_of[3], (IMAGES, SEQ, E), 1.0, 6.0, ((0, 256),)),
        "weight_codes": bell_draw(key_of[4], (ROWS, E), 1.0, 4.0, ((0, 32),)),
        "weight_scales": jnp.clip(jnp.exp(math.log(0.06) - 2.3025851 * jax.random.uniform(key_of[5], (ROWS, E // BLOCK), jnp.float32) ** block_levels(key_of[5], (ROWS, E // BLOCK), ((0, 32),), -0.2, 0.2)), 0.006, 0.06),
    }


def forward_image(arrays_in):
    query, keyset, valueset = arrays_in
    seq_len = query.shape[0]
    query_heads = query.astype(jnp.float32).reshape(seq_len, H, HD)
    key_heads = keyset.astype(jnp.float32).reshape(seq_len, H, HD)
    value_heads = valueset.astype(jnp.float32).reshape(seq_len, H, HD)
    scores = jnp.einsum("qhd,khd->hqk", query_heads, key_heads) * HD ** -0.5
    highest = jnp.max(scores, axis=2, keepdims=True)
    exponent = jnp.exp(scores - highest)
    probability = exponent / jnp.sum(exponent, axis=2, keepdims=True)
    weight_half = probability.astype(jnp.bfloat16)
    context = jnp.einsum("hqk,khd->qhd", weight_half.astype(jnp.float32), value_heads).astype(jnp.bfloat16)
    return probability, weight_half, context.reshape(seq_len, H * HD)


def context_only(arrays_in):
    return forward_image(arrays_in)[2]


def backward_image(arrays_in):
    query, keyset, valueset, grad_context = arrays_in
    seq_len = query.shape[0]
    probability, weight_half, context = forward_image((query, keyset, valueset))
    query_heads = query.astype(jnp.float32).reshape(seq_len, H, HD)
    key_heads = keyset.astype(jnp.float32).reshape(seq_len, H, HD)
    value_heads = valueset.astype(jnp.float32).reshape(seq_len, H, HD)
    grad_heads = grad_context.astype(jnp.float32).reshape(seq_len, H, HD)
    grad_value = jnp.einsum("hqk,qhd->khd", weight_half.astype(jnp.float32), grad_heads).astype(jnp.bfloat16)
    dprobs = jnp.einsum("qhd,khd->hqk", grad_heads, value_heads)
    row_delta = jnp.sum(probability * dprobs, axis=2, keepdims=True)
    dscores = (probability * (dprobs - row_delta) * HD ** -0.5).astype(jnp.bfloat16).astype(jnp.float32)
    grad_query = jnp.einsum("hqk,khd->qhd", dscores, key_heads).astype(jnp.bfloat16)
    grad_key = jnp.einsum("hqk,qhd->khd", dscores, query_heads).astype(jnp.bfloat16)
    return (grad_query.reshape(seq_len, H * HD), grad_key.reshape(seq_len, H * HD), grad_value.reshape(seq_len, H * HD))


def reference(queries, keys, values, grad_output, weight_codes, weight_scales):
    scaled = weight_codes.astype(jnp.float32).reshape(ROWS, E // BLOCK, BLOCK) * weight_scales[:, :, None]
    weight = scaled.reshape(ROWS, E).astype(jnp.bfloat16)
    contexts = lax.map(context_only, (queries, keys, values))
    grad_flat = jnp.dot(grad_output.reshape(IMAGES * SEQ, E), weight.T, preferred_element_type=jnp.float32)
    grad_context = grad_flat.astype(jnp.bfloat16).reshape(IMAGES, SEQ, ROWS)
    block_total = N_GROUP * N_REP
    context_blocks = contexts.reshape(block_total, IMG_DEV * SEQ, ROWS)
    output_blocks = grad_output.reshape(block_total, IMG_DEV * SEQ, E)

    def add_block(running, pair):
        term = jnp.dot(pair[0].T, pair[1], preferred_element_type=jnp.float32).astype(jnp.bfloat16)
        return running + lax.optimization_barrier(term).astype(jnp.float32), None

    grad_weight, unused = lax.scan(add_block, jnp.zeros((ROWS, E), jnp.float32), (context_blocks, output_blocks))
    grad_queries, grad_keys, grad_values = lax.map(backward_image, (queries, keys, values, grad_context))
    return grad_queries, grad_keys, grad_values, grad_weight
```

```python
import functools

import jax
import jax.numpy as jnp
from jax import lax
from jax.experimental import pallas as pl
from jax.experimental.pallas import tpu as pltpu
from jax.sharding import Mesh
from jax.sharding import PartitionSpec as P

AXES = ("zh", "zl", "xl", "c", "xh", "y")
SHARD = ("zh", "zl", "xl", "c")
HD = 128
SCALE = HD**-0.5
F32 = jnp.float32
BF16 = jnp.bfloat16
SWAP = [(0, 1), (1, 0)]
NT = (((1,), (1,)), ((), ()))
TN = (((0,), (0,)), ((), ()))
VMEM_LIMIT = 50 * 2**20


def ring(count, step):
    return [(i, (i + step) % count) for i in range(count)]


def x_ring(step):
    def place(x):
        return (x % 2) * 2 + x // 2

    return [(place(x), place((x + step) % 4)) for x in range(4)]


def dot(a, b, dims):
    return lax.dot_general(a, b, dims, preferred_element_type=F32)


def params():
    return pltpu.CompilerParams(
        dimension_semantics=("arbitrary",), vmem_limit_bytes=VMEM_LIMIT
    )


def cost(flops, moved, exps=0):
    return pl.CostEstimate(flops=flops, bytes_accessed=moved, transcendentals=exps)


def softmax(q, k):
    scores = dot(q, k, NT) * SCALE
    exponent = jnp.exp(scores - jnp.max(scores, axis=1, keepdims=True))
    return exponent * (1.0 / jnp.sum(exponent, axis=1, keepdims=True))


def forward_body(pick, q_ref, k_ref, v_ref, out_ref):
    for head in range(q_ref.shape[1] // HD):
        cols = slice(head * HD, (head + 1) * HD)
        probs = softmax(q_ref[:, cols], k_ref[:, cols]).astype(BF16)
        context_t = dot(v_ref[:, cols], probs, (((0,), (1,)), ((), ())))
        out_ref[cols, :] = context_t.astype(BF16)


def forward(parity, q, k, v, width):
    seq, total = q.shape
    blocks = total // width // 2
    spec = pl.BlockSpec((seq, width), lambda i, pick: (0, 2 * i + pick[0]))
    return pl.pallas_call(
        forward_body,
        grid_spec=pltpu.PrefetchScalarGridSpec(
            num_scalar_prefetch=1,
            grid=(blocks,),
            in_specs=[spec] * 3,
            out_specs=pl.BlockSpec((width, seq), lambda i, pick: (i, 0)),
        ),
        out_shape=jax.ShapeDtypeStruct((total // 2, seq), BF16),
        compiler_params=params(),
        cost_estimate=cost(2 * seq * seq * total, 2 * seq * total * 2, seq * seq * total // HD // 2),
        name="context_half",
    )(parity, q, k, v)


def backward_body(own, pick, q_ref, k_ref, v_ref, *refs):
    if own:
        g_ref, r_ref, gq_ref, gk_ref, gv_ref = refs
    else:
        g_ref, _, _, _, gq_ref, gk_ref, gv_ref = refs
    for head in range(q_ref.shape[1] // HD):
        cols = slice(head * HD, (head + 1) * HD)
        q, k, v = q_ref[:, cols], k_ref[:, cols], v_ref[:, cols]
        if own:
            g = (g_ref[:, cols] + r_ref[:, cols].astype(F32)).astype(BF16)
        else:
            g = g_ref[:, cols]
        probs = softmax(q, k)
        gv_ref[:, cols] = dot(probs.astype(BF16), g, TN).astype(BF16)
        dprobs = dot(g, v, NT)
        delta = jnp.sum(probs * dprobs, axis=1, keepdims=True)
        dscores = (probs * (dprobs - delta) * SCALE).astype(BF16)
        gq_ref[:, cols] = dot(dscores, k, (((1,), (0,)), ((), ()))).astype(BF16)
        gk_ref[:, cols] = dot(dscores, q, TN).astype(BF16)


def backward(parity, q, k, v, grads, width, before=None):
    seq, total = q.shape
    blocks = total // width // 2
    spec = pl.BlockSpec((seq, width), lambda i, pick: (0, 2 * i + pick[0]))
    half = pl.BlockSpec((seq, width), lambda i, pick: (0, i))
    whole = jax.ShapeDtypeStruct((seq, total), BF16)
    extra = [] if before is None else list(before)
    return pl.pallas_call(
        functools.partial(backward_body, before is None),
        grid_spec=pltpu.PrefetchScalarGridSpec(
            num_scalar_prefetch=1,
            grid=(blocks,),
            in_specs=[spec] * 3
            + [half] * len(grads)
            + [pl.BlockSpec(memory_space=pl.ANY)] * len(extra),
            out_specs=[spec] * 3,
        ),
        out_shape=[whole] * 3,
        input_output_aliases={} if before is None else {5: 0, 6: 1, 7: 2},
        compiler_params=params(),
        cost_estimate=cost(5 * seq * seq * total, 7 * seq * total, seq * seq * total // HD // 2),
        name="attention_gradients",
    )(parity, q, k, v, *grads, *extra)


def restore_body(place, codes_ref, scales_ref, out_ref):
    index = (place[pl.program_id(0)] * 3 + pl.program_id(1)) // 2
    scales = scales_ref[...]
    lanes = lax.broadcasted_iota(jnp.int32, scales.shape, 1)
    scale = jnp.sum(jnp.where(lanes == index, scales, 0.0), axis=1, keepdims=True)
    out_ref[0] = (codes_ref[...].astype(F32) * scale).astype(BF16)


def restore(places, codes, scales):
    rows = codes.shape[0]
    return pl.pallas_call(
        restore_body,
        grid_spec=pltpu.PrefetchScalarGridSpec(
            num_scalar_prefetch=1,
            grid=(2, 3),
            in_specs=[
                pl.BlockSpec((rows, 128), lambda h, j, place: (0, place[h] * 3 + j)),
                pl.BlockSpec(scales.shape, lambda h, j, place: (0, 0)),
            ],
            out_specs=pl.BlockSpec((1, rows, 128), lambda h, j, place: (h, 0, j)),
        ),
        out_shape=jax.ShapeDtypeStruct((2, rows, 384), BF16),
        cost_estimate=cost(rows * 768, rows * 3072),
        name="weight_pieces",
    )(places, codes, scales)


def context_gradient_body(place, d0, d1, d2, d3, w0, w1, w2, wa, wb, g0, g1, g2, g3):
    far = jnp.where(pl.program_id(0) < 2, wa[...], wb[...])
    width = w0.shape[1]
    total = None
    for part, weight in enumerate((w0[...], w1[...], w2[...], far)):
        cols = pl.ds(pl.multiple_of(place[part] * width, 128), width)
        rows = jnp.concatenate([d[:, cols] for d in (d0, d1, d2, d3)], axis=0)
        term = dot(rows, weight, NT)
        total = term if total is None else total + term
    seq = d0.shape[0]
    for image, out in enumerate((g0, g1, g2, g3)):
        out[...] = total[image * seq : (image + 1) * seq].astype(out.dtype)


def context_gradient(places, grads, weights):
    seq, features = grads[0].shape
    rows = weights[0].shape[0]
    width = weights[0].shape[1]
    block = rows // 4
    full = pl.BlockSpec((seq, features), lambda i, place: (0, 0))
    by_row = pl.BlockSpec((block, width), lambda i, place: (i, 0))
    out = pl.BlockSpec((seq, block), lambda i, place: (0, i))
    return pl.pallas_call(
        context_gradient_body,
        grid_spec=pltpu.PrefetchScalarGridSpec(
            num_scalar_prefetch=1,
            grid=(4,),
            in_specs=[full] * 4
            + [by_row] * 3
            + [
                pl.BlockSpec((block, width), lambda i, place: (jnp.minimum(i, 1), 0)),
                pl.BlockSpec((block, width), lambda i, place: (jnp.maximum(i - 2, 0), 0)),
            ],
            out_specs=[out] * 4,
        ),
        out_shape=[
            jax.ShapeDtypeStruct((seq, rows), kind) for kind in (F32, BF16, F32, BF16)
        ],
        compiler_params=params(),
        cost_estimate=cost(8 * seq * features * rows, 20 * 2**20),
        name="context_gradient",
    )(places, *grads, *weights)


def weight_gradient_body(c0, c1, c2, c3, d0, d1, d2, d3, out_ref):
    total = None
    for context_t, grad in ((c0, d0), (c1, d1), (c2, d2), (c3, d3)):
        term = dot(context_t[...], grad[...], (((1,), (0,)), ((), ())))
        total = term if total is None else total + term
    for xl in range(2):
        for core in range(2):
            for xh in range(2):
                first = (xl * 2 + core) * 96 + xh * 48
                for y in range(4):
                    piece = total[first : first + 48, y * 384 : (y + 1) * 384]
                    out_ref[xl, xh, y, 0, core] = piece.astype(BF16)


def weight_gradient(contexts, grads):
    rows, seq = contexts[0].shape
    features = grads[0].shape[1]
    return pl.pallas_call(
        weight_gradient_body,
        grid=(4,),
        in_specs=[pl.BlockSpec((rows // 4, seq), lambda i: (i, 0))] * 4
        + [pl.BlockSpec((seq, features), lambda i: (0, 0))] * 4,
        out_specs=pl.BlockSpec((2, 2, 4, 1, 2, 48, 384), lambda i: (0, 0, 0, i, 0, 0, 0)),
        out_shape=jax.ShapeDtypeStruct((2, 2, 4, 4, 2, 48, 384), BF16),
        compiler_params=params(),
        cost_estimate=cost(8 * seq * features * rows, 16 * 2**20),
        name="weight_gradient",
    )(*contexts, *grads)


def per_device(queries, keys, values, grad_output, weight_codes, weight_scales):
    _, seq, total = queries.shape
    features = grad_output.shape[2]
    q, k, v = (a.reshape(seq, total) for a in (queries, keys, values))
    grad = grad_output.reshape(seq, features)
    zh, zl, xl, c, y = (lax.axis_index(name) for name in ("zh", "zl", "xl", "c", "y"))
    half = features // 2
    width = 384
    own_parity = zl.astype(jnp.int32).reshape(1)
    other_parity = 1 - own_parity

    d0 = lax.dynamic_slice_in_dim(grad, c * half, half, 1)
    d1 = lax.ppermute(lax.dynamic_slice_in_dim(grad, (1 - c) * half, half, 1), "c", SWAP)
    d2 = lax.ppermute(d0, "zl", SWAP)
    d3 = lax.ppermute(d1, "zl", SWAP)
    grads = (d0, d1, d2, d3)

    places = jnp.stack([c * 4 + y, (1 - c) * 4 + y]).astype(jnp.int32)
    pieces = restore(places, weight_codes, weight_scales)
    arrived = lax.ppermute(pieces[1], "c", SWAP)
    pair = jnp.where(
        c == 0,
        jnp.concatenate([pieces[0], arrived], 0),
        jnp.concatenate([arrived, pieces[0]], 0),
    )
    from_behind = [lax.ppermute(pair, "zh", ring(4, step)) for step in (1, 2, 3)]
    turned = [pair, from_behind[2], from_behind[1], from_behind[0]]
    column = lax.dynamic_slice_in_dim(jnp.stack(turned + turned), (4 - zh) % 4, 4, 0)
    beside = jnp.concatenate(
        [
            lax.ppermute(column[:2], ("xl", "xh"), x_ring(1)),
            lax.ppermute(column[2:], ("xl", "xh"), x_ring(-1)),
        ],
        0,
    )
    here = jnp.where(xl == 0, jnp.stack([column, beside], 1), jnp.stack([beside, column], 1))
    here = here.reshape(-1, width)
    rows = here.shape[0]
    below = lax.ppermute(here, "y", ring(4, 1))
    above = lax.ppermute(here, "y", ring(4, -1))
    far_a = lax.ppermute(below[: rows // 2], "y", ring(4, 1))
    far_b = lax.ppermute(above[rows // 2 :], "y", ring(4, -1))

    context_other = forward(other_parity, q, k, v, width)
    c2 = lax.ppermute(context_other, "zl", SWAP)
    context_own = forward(own_parity, q, k, v, width)
    c1 = lax.ppermute(context_own, "c", SWAP)
    c3 = lax.ppermute(c2, "c", SWAP)
    terms = weight_gradient((context_own, c1, c2, c3), grads)
    terms = lax.all_to_all(
        terms.reshape(16, 8, 48, width), ("xl", "xh", "y"), 0, 0, tiled=True
    )
    sums = jnp.sum(terms.astype(F32), axis=0).astype(BF16)
    sums = lax.all_to_all(sums.reshape(32, 12, width), ("zh", "c", "y"), 0, 0, tiled=True)
    grad_weight = jnp.sum(sums.astype(F32).reshape(4, 8, 12, width), axis=0)
    grad_weight = jnp.moveaxis(grad_weight, 0, 1).reshape(12, features)

    places = jnp.stack([y, (y + 3) % 4, (y + 1) % 4, (y + 2) % 4]).astype(jnp.int32)
    g0, g1, g2, g3 = context_gradient(places, grads, (here, below, above, far_a, far_b))
    r3 = lax.ppermute(g3, "c", SWAP)
    r1 = lax.ppermute(g1, "c", SWAP)
    g_other = lax.ppermute((g2 + r3.astype(F32)).astype(BF16), "zl", SWAP)
    first = backward(own_parity, q, k, v, (g0, r1), width)
    outs = backward(other_parity, q, k, v, (g_other,), width, first)
    return tuple(out.reshape(1, seq, total) for out in outs) + (grad_weight,)


def solution(mesh):
    split = Mesh(mesh.devices.reshape(4, 2, 2, 2, 2, 4), AXES)
    image = P(AXES, None, None)
    return jax.shard_map(
        per_device,
        mesh=split,
        in_specs=(image, image, image, image, P(SHARD, None), P(SHARD, None)),
        out_specs=(image, image, image, P(AXES, None)),
        check_vma=False,
    )
```

```python
import functools

import jax
import jax.numpy as jnp
from jax import lax
from jax.experimental import pallas as pl
from jax.experimental.pallas import tpu as pltpu
from jax.sharding import Mesh
from jax.sharding import PartitionSpec as P

AXES = ("zh", "zl", "xl", "c", "xh", "y")
SHARD = ("zh", "zl", "xl", "c")
HD = 128
SCALE = HD**-0.5
F32 = jnp.float32
BF16 = jnp.bfloat16
SWAP = [(0, 1), (1, 0)]
NT = (((1,), (1,)), ((), ()))
TN = (((0,), (0,)), ((), ()))
VMEM_LIMIT = 50 * 2**20


def ring(count, step):
    return [(i, (i + step) % count) for i in range(count)]


def x_ring(step):
    def place(x):
        return (x % 2) * 2 + x // 2

    return [(place(x), place((x + step) % 4)) for x in range(4)]


def dot(a, b, dims):
    return lax.dot_general(a, b, dims, preferred_element_type=F32)


def params():
    return pltpu.CompilerParams(
        dimension_semantics=("arbitrary",), vmem_limit_bytes=VMEM_LIMIT
    )


def cost(flops, moved, exps=0):
    return pl.CostEstimate(flops=flops, bytes_accessed=moved, transcendentals=exps)


def softmax(q, k):
    scores = dot(q, k, NT) * SCALE
    exponent = jnp.exp(scores - jnp.max(scores, axis=1, keepdims=True))
    return exponent * (1.0 / jnp.sum(exponent, axis=1, keepdims=True))


def forward_body(pick, q_ref, k_ref, v_ref, out_ref):
    for head in range(q_ref.shape[1] // HD):
        cols = slice(head * HD, (head + 1) * HD)
        probs = softmax(q_ref[:, cols], k_ref[:, cols]).astype(BF16)
        context_t = dot(v_ref[:, cols], probs, (((0,), (1,)), ((), ())))
        out_ref[cols, :] = context_t.astype(BF16)


def forward(parity, q, k, v, width):
    seq, total = q.shape
    blocks = total // width // 2
    spec = pl.BlockSpec((seq, width), lambda i, pick: (0, 2 * i + pick[0]))
    return pl.pallas_call(
        forward_body,
        grid_spec=pltpu.PrefetchScalarGridSpec(
            num_scalar_prefetch=1,
            grid=(blocks,),
            in_specs=[spec] * 3,
            out_specs=pl.BlockSpec((width, seq), lambda i, pick: (i, 0)),
        ),
        out_shape=jax.ShapeDtypeStruct((total // 2, seq), BF16),
        compiler_params=params(),
        cost_estimate=cost(2 * seq * seq * total, 2 * seq * total * 2, seq * seq * total // HD // 2),
        name="context_half",
    )(parity, q, k, v)


def backward_body(own, pick, q_ref, k_ref, v_ref, *refs):
    if own:
        g_ref, r_ref, gq_ref, gk_ref, gv_ref = refs
    else:
        g_ref, _, _, _, gq_ref, gk_ref, gv_ref = refs
    for head in range(q_ref.shape[1] // HD):
        cols = slice(head * HD, (head + 1) * HD)
        q, k, v = q_ref[:, cols], k_ref[:, cols], v_ref[:, cols]
        if own:
            g = (g_ref[:, cols] + r_ref[:, cols].astype(F32)).astype(BF16)
        else:
            g = g_ref[:, cols]
        probs = softmax(q, k)
        gv_ref[:, cols] = dot(probs.astype(BF16), g, TN).astype(BF16)
        dprobs = dot(g, v, NT)
        delta = jnp.sum(probs * dprobs, axis=1, keepdims=True)
        dscores = (probs * (dprobs - delta) * SCALE).astype(BF16)
        gq_ref[:, cols] = dot(dscores, k, (((1,), (0,)), ((), ()))).astype(BF16)
        gk_ref[:, cols] = dot(dscores, q, TN).astype(BF16)


def backward(parity, q, k, v, grads, width, before=None):
    seq, total = q.shape
    blocks = total // width // 2
    spec = pl.BlockSpec((seq, width), lambda i, pick: (0, 2 * i + pick[0]))
    half = pl.BlockSpec((seq, width), lambda i, pick: (0, i))
    whole = jax.ShapeDtypeStruct((seq, total), BF16)
    extra = [] if before is None else list(before)
    return pl.pallas_call(
        functools.partial(backward_body, before is None),
        grid_spec=pltpu.PrefetchScalarGridSpec(
            num_scalar_prefetch=1,
            grid=(blocks,),
            in_specs=[spec] * 3
            + [half] * len(grads)
            + [pl.BlockSpec(memory_space=pl.ANY)] * len(extra),
            out_specs=[spec] * 3,
        ),
        out_shape=[whole] * 3,
        input_output_aliases={} if before is None else {5: 0, 6: 1, 7: 2},
        compiler_params=params(),
        cost_estimate=cost(5 * seq * seq * total, 7 * seq * total, seq * seq * total // HD // 2),
        name="attention_gradients",
    )(parity, q, k, v, *grads, *extra)


def after(values, events):
    return lax.optimization_barrier((values, events))[0]


def restore_body(place, codes_ref, scales_ref, near_ref, away_ref):
    scales = scales_ref[...]
    lanes = lax.broadcasted_iota(jnp.int32, scales.shape, 1)
    for part, out in enumerate((near_ref, away_ref)):
        for tile in range(out.shape[1] // 128):
            column = place[part] * (out.shape[1] // 128) + tile
            codes = codes_ref[:, pl.ds(pl.multiple_of(column * 128, 128), 128)].astype(F32)
            chosen = jnp.where(lanes == column // 2, scales, 0.0)
            scale = jnp.sum(chosen, axis=1, keepdims=True)
            out[:, tile * 128 : (tile + 1) * 128] = (codes * scale).astype(BF16)


def restore(places, codes, scales):
    rows = codes.shape[0]
    return pl.pallas_call(
        restore_body,
        in_specs=[
            pl.BlockSpec(memory_space=pltpu.SMEM),
            pl.BlockSpec(memory_space=pltpu.VMEM),
            pl.BlockSpec(memory_space=pltpu.VMEM),
        ],
        out_shape=[jax.ShapeDtypeStruct((rows, 384), BF16)] * 2,
        cost_estimate=cost(rows * 768, rows * 3072),
        name="weight_pieces",
    )(places, codes, scales)


def context_gradient_body(place, d0, d1, d2, d3, w0, w1, w2, wa, wb, g0, g1, g2, g3):
    far = jnp.where(pl.program_id(0) < 2, wa[...], wb[...])
    width = w0.shape[1]
    seq = d0.shape[0]
    weight = jnp.concatenate([w0[...], w1[...], w2[...], far], axis=1)
    columns = []
    for part in range(4):
        cols = pl.ds(pl.multiple_of(place[part] * width, 128), width)
        columns.append(jnp.concatenate([d[:, cols] for d in (d0, d1, d2, d3)], axis=0))
    total = dot(jnp.concatenate(columns, axis=1), weight, NT)
    for image, out in enumerate((g0, g1, g2, g3)):
        out[...] = total[image * seq : (image + 1) * seq].astype(out.dtype)


def context_gradient(places, grads, weights):
    seq, features = grads[0].shape
    rows = weights[0].shape[0]
    width = weights[0].shape[1]
    block = rows // 4
    full = pl.BlockSpec((seq, features), lambda i, place: (0, 0))
    by_row = pl.BlockSpec((block, width), lambda i, place: (i, 0))
    out = pl.BlockSpec((seq, block), lambda i, place: (0, i))
    return pl.pallas_call(
        context_gradient_body,
        grid_spec=pltpu.PrefetchScalarGridSpec(
            num_scalar_prefetch=1,
            grid=(4,),
            in_specs=[full] * 4
            + [by_row] * 3
            + [
                pl.BlockSpec((block, width), lambda i, place: (jnp.minimum(i, 1), 0)),
                pl.BlockSpec((block, width), lambda i, place: (jnp.maximum(i - 2, 0), 0)),
            ],
            out_specs=[out] * 4,
        ),
        out_shape=[
            jax.ShapeDtypeStruct((seq, rows), kind) for kind in (F32, BF16, F32, BF16)
        ],
        compiler_params=params(),
        cost_estimate=cost(8 * seq * features * rows, 20 * 2**20),
        name="context_gradient",
    )(places, *grads, *weights)


def weight_gradient_body(c0, c1, c2, c3, d0, d1, d2, d3, out_ref):
    context_t = jnp.concatenate([c[...] for c in (c0, c1, c2, c3)], axis=1)
    for y in range(4):
        grad = jnp.concatenate([d[:, y * 384 : (y + 1) * 384] for d in (d0, d1, d2, d3)], axis=0)
        total = dot(context_t, grad, (((1,), (0,)), ((), ())))
        for xl in range(2):
            for core in range(2):
                for xh in range(2):
                    first = (xl * 2 + core) * 96 + xh * 48
                    out_ref[xl, xh, y, 0, core] = total[first : first + 48].astype(BF16)


def weight_gradient(contexts, grads):
    rows, seq = contexts[0].shape
    features = grads[0].shape[1]
    return pl.pallas_call(
        weight_gradient_body,
        grid=(4,),
        in_specs=[pl.BlockSpec((rows // 4, seq), lambda i: (i, 0))] * 4
        + [pl.BlockSpec((seq, features), lambda i: (0, 0))] * 4,
        out_specs=pl.BlockSpec((2, 2, 4, 1, 2, 48, 384), lambda i: (0, 0, 0, i, 0, 0, 0)),
        out_shape=jax.ShapeDtypeStruct((2, 2, 4, 4, 2, 48, 384), BF16),
        compiler_params=params(),
        cost_estimate=cost(8 * seq * features * rows, 16 * 2**20),
        name="weight_gradient",
    )(*contexts, *grads)


def per_device(queries, keys, values, grad_output, weight_codes, weight_scales):
    _, seq, total = queries.shape
    features = grad_output.shape[2]
    q, k, v = (a.reshape(seq, total) for a in (queries, keys, values))
    grad = grad_output.reshape(seq, features)
    zh, zl, xl, c, y = (lax.axis_index(name) for name in ("zh", "zl", "xl", "c", "y"))
    half = features // 2
    width = 384
    own_parity = zl.astype(jnp.int32).reshape(1)
    other_parity = 1 - own_parity

    d0 = lax.dynamic_slice_in_dim(grad, c * half, half, 1)
    d1 = lax.ppermute(lax.dynamic_slice_in_dim(grad, (1 - c) * half, half, 1), "c", SWAP)
    d2 = lax.ppermute(d0, "zl", SWAP)

    places = jnp.stack([c * 4 + y, (1 - c) * 4 + y]).astype(jnp.int32)
    pieces = restore(places, weight_codes, weight_scales)
    arrived = lax.ppermute(pieces[1], "c", SWAP)
    pair = jnp.where(
        c == 0,
        jnp.concatenate([pieces[0], arrived], 0),
        jnp.concatenate([arrived, pieces[0]], 0),
    )
    from_behind = [lax.ppermute(pair, "zh", ring(4, step)) for step in (1, 2, 3)]
    turned = [pair, from_behind[2], from_behind[1], from_behind[0]]
    column = lax.dynamic_slice_in_dim(jnp.stack(turned + turned), (4 - zh) % 4, 4, 0)
    context_other = forward(other_parity, q, k, v, width)
    (context_other,) = after((context_other,), (column, d2))
    c2 = lax.ppermute(context_other, "zl", SWAP)
    (d1,) = after((d1,), (c2,))
    d3 = lax.ppermute(d1, "zl", SWAP)
    grads = (d0, d1, d2, d3)
    beside = jnp.concatenate(
        [
            lax.ppermute(column[:2], ("xl", "xh"), x_ring(1)),
            lax.ppermute(column[2:], ("xl", "xh"), x_ring(-1)),
        ],
        0,
    )
    here = jnp.where(xl == 0, jnp.stack([column, beside], 1), jnp.stack([beside, column], 1))
    here = here.reshape(-1, width)
    rows = here.shape[0]
    below = lax.ppermute(here, "y", ring(4, 1))
    above = lax.ppermute(here, "y", ring(4, -1))
    far_a = lax.ppermute(below[: rows // 2], "y", ring(4, 1))
    far_b = lax.ppermute(above[rows // 2 :], "y", ring(4, -1))

    context_own = forward(own_parity, q, k, v, width)
    c1 = lax.ppermute(context_own, "c", SWAP)
    (c2,) = after((c2,), (here,))
    c3 = lax.ppermute(c2, "c", SWAP)
    (c3,) = after((c3,), (below, above))
    terms = weight_gradient((context_own, c1, c2, c3), grads)
    (terms,) = after((terms,), (far_a, far_b))
    terms = lax.all_to_all(
        terms.reshape(16, 8, 48, width), ("xl", "xh", "y"), 0, 0, tiled=True
    )

    places = jnp.stack([y, (y + 3) % 4, (y + 1) % 4, (y + 2) % 4]).astype(jnp.int32)
    g0, g1, g2, g3 = context_gradient(places, grads, (here, below, above, far_a, far_b))
    r3 = lax.ppermute(g3, "c", SWAP)
    r1 = lax.ppermute(g1, "c", SWAP)
    g_other = lax.ppermute((g2 + r3.astype(F32)).astype(BF16), "zl", SWAP)
    first = backward(own_parity, q, k, v, (g0, r1), width)
    outs = backward(other_parity, q, k, v, (g_other,), width, first)

    (terms,) = after((terms,), tuple(outs))
    sums = jnp.sum(terms.astype(F32), axis=0).astype(BF16)
    sums = lax.all_to_all(sums.reshape(32, 12, width), ("zh", "c", "y"), 0, 0, tiled=True)
    grad_weight = jnp.sum(sums.astype(F32).reshape(4, 8, 12, width), axis=0)
    grad_weight = jnp.moveaxis(grad_weight, 0, 1).reshape(12, features)
    return tuple(out.reshape(1, seq, total) for out in outs) + (grad_weight,)


def solution(mesh):
    split = Mesh(mesh.devices.reshape(4, 2, 2, 2, 2, 4), AXES)
    image = P(AXES, None, None)
    return jax.shard_map(
        per_device,
        mesh=split,
        in_specs=(image, image, image, image, P(SHARD, None), P(SHARD, None)),
        out_specs=(image, image, image, P(AXES, None)),
        check_vma=False,
    )
```

```python
import functools

import jax
import jax.numpy as jnp
from jax import lax
from jax.experimental import pallas as pl
from jax.experimental.pallas import tpu as pltpu
from jax.sharding import Mesh
from jax.sharding import PartitionSpec as P

AXES = ("zh", "zl", "xl", "c", "xh", "y")
SHARD = ("zh", "zl", "xl", "c")
HD = 128
SCALE = HD**-0.5
F32 = jnp.float32
BF16 = jnp.bfloat16
SWAP = [(0, 1), (1, 0)]
NT = (((1,), (1,)), ((), ()))
TN = (((0,), (0,)), ((), ()))
VMEM_LIMIT = 50 * 2**20


def ring(count, step):
    return [(i, (i + step) % count) for i in range(count)]


def x_ring(step):
    def place(x):
        return (x % 2) * 2 + x // 2

    return [(place(x), place((x + step) % 4)) for x in range(4)]


def dot(a, b, dims):
    return lax.dot_general(a, b, dims, preferred_element_type=F32)


def params():
    return pltpu.CompilerParams(
        dimension_semantics=("arbitrary",), vmem_limit_bytes=VMEM_LIMIT
    )


def cost(flops, moved, exps=0):
    return pl.CostEstimate(flops=flops, bytes_accessed=moved, transcendentals=exps)


def softmax(q, k):
    scores = dot(q, k, NT) * SCALE
    exponent = jnp.exp(scores - jnp.max(scores, axis=1, keepdims=True))
    return exponent * (1.0 / jnp.sum(exponent, axis=1, keepdims=True))


def forward_body(pick, q_ref, k_ref, v_ref, out_ref, plain, sorted_rows):
    for head in range(q_ref.shape[1] // HD):
        cols = slice(head * HD, (head + 1) * HD)
        probs = softmax(q_ref[:, cols], k_ref[:, cols]).astype(BF16)
        plain[cols, :] = dot(v_ref[:, cols], probs, (((0,), (1,)), ((), ())))
    for xl in range(2):
        for xh in range(2):
            for y in range(4):
                for core in range(2):
                    old = xl * 192 + core * 96 + xh * 48 + y * 12
                    new = xl * 192 + xh * 96 + y * 24 + core * 12
                    sorted_rows[new : new + 12, :] = plain[old : old + 12, :]
    out_ref[...] = sorted_rows[...].astype(BF16)


def forward(parity, q, k, v, width):
    seq, total = q.shape
    blocks = total // width // 2
    spec = pl.BlockSpec((seq, width), lambda i, pick: (0, 2 * i + pick[0]))
    return pl.pallas_call(
        forward_body,
        grid_spec=pltpu.PrefetchScalarGridSpec(
            num_scalar_prefetch=1,
            grid=(blocks,),
            in_specs=[spec] * 3,
            out_specs=pl.BlockSpec((width, seq), lambda i, pick: (i, 0)),
            scratch_shapes=[pltpu.VMEM((width, seq), F32)] * 2,
        ),
        out_shape=jax.ShapeDtypeStruct((total // 2, seq), BF16),
        compiler_params=params(),
        cost_estimate=cost(2 * seq * seq * total, 2 * seq * total * 2, seq * seq * total // HD // 2),
        name="context_half",
    )(parity, q, k, v)


def backward_body(own, pick, q_ref, k_ref, v_ref, *refs):
    if own:
        g_ref, r_ref, gq_ref, gk_ref, gv_ref = refs
    else:
        g_ref, _, _, _, gq_ref, gk_ref, gv_ref = refs
    for head in range(q_ref.shape[1] // HD):
        cols = slice(head * HD, (head + 1) * HD)
        q, k, v = q_ref[:, cols], k_ref[:, cols], v_ref[:, cols]
        if own:
            g = (g_ref[:, cols] + r_ref[:, cols].astype(F32)).astype(BF16)
        else:
            g = g_ref[:, cols]
        probs = softmax(q, k)
        gv_ref[:, cols] = dot(probs.astype(BF16), g, TN).astype(BF16)
        dprobs = dot(g, v, NT)
        delta = jnp.sum(probs * dprobs, axis=1, keepdims=True)
        dscores = (probs * (dprobs - delta) * SCALE).astype(BF16)
        gq_ref[:, cols] = dot(dscores, k, (((1,), (0,)), ((), ()))).astype(BF16)
        gk_ref[:, cols] = dot(dscores, q, TN).astype(BF16)


def backward(parity, q, k, v, grads, width, before=None):
    seq, total = q.shape
    blocks = total // width // 2
    spec = pl.BlockSpec((seq, width), lambda i, pick: (0, 2 * i + pick[0]))
    half = pl.BlockSpec((seq, width), lambda i, pick: (0, i))
    whole = jax.ShapeDtypeStruct((seq, total), BF16)
    extra = [] if before is None else list(before)
    return pl.pallas_call(
        functools.partial(backward_body, before is None),
        grid_spec=pltpu.PrefetchScalarGridSpec(
            num_scalar_prefetch=1,
            grid=(blocks,),
            in_specs=[spec] * 3
            + [half] * len(grads)
            + [pl.BlockSpec(memory_space=pl.ANY)] * len(extra),
            out_specs=[spec] * 3,
        ),
        out_shape=[whole] * 3,
        input_output_aliases={} if before is None else {5: 0, 6: 1, 7: 2},
        compiler_params=params(),
        cost_estimate=cost(5 * seq * seq * total, 7 * seq * total, seq * seq * total // HD // 2),
        name="attention_gradients",
    )(parity, q, k, v, *grads, *extra)


def after(values, events):
    return lax.optimization_barrier((values, events))[0]


def restore_body(place, codes_ref, scales_ref, near_ref, away_ref):
    scales = scales_ref[...]
    lanes = lax.broadcasted_iota(jnp.int32, scales.shape, 1)
    for part, out in enumerate((near_ref, away_ref)):
        for tile in range(out.shape[1] // 128):
            column = place[part] * (out.shape[1] // 128) + tile
            codes = codes_ref[:, pl.ds(pl.multiple_of(column * 128, 128), 128)].astype(F32)
            chosen = jnp.where(lanes == column // 2, scales, 0.0)
            scale = jnp.sum(chosen, axis=1, keepdims=True)
            out[:, tile * 128 : (tile + 1) * 128] = (codes * scale).astype(BF16)


def restore(places, codes, scales):
    rows = codes.shape[0]
    return pl.pallas_call(
        restore_body,
        in_specs=[
            pl.BlockSpec(memory_space=pltpu.SMEM),
            pl.BlockSpec(memory_space=pltpu.VMEM),
            pl.BlockSpec(memory_space=pltpu.VMEM),
        ],
        out_shape=[jax.ShapeDtypeStruct((rows, 384), BF16)] * 2,
        cost_estimate=cost(rows * 768, rows * 3072),
        name="weight_pieces",
    )(places, codes, scales)


def four_images(near, away):
    return jnp.concatenate([near[0], near[1], away[0], away[1]], axis=0)


def context_gradient_body(place, a0, a1, b0, b1, w0, w1, w2, wa, wb, g0, g1, g2, g3, rows_ref):
    far = jnp.where(pl.program_id(0) < 2, wa[...], wb[...])
    width = w0.shape[1]
    seq = a0.shape[1]
    for part, weight in enumerate((w0[...], w1[...], w2[...], far)):
        rows_ref[:, pl.ds(pl.multiple_of(place[part] * width, 128), width)] = weight
    grads = jnp.concatenate([four_images(a0, a1), four_images(b0, b1)], axis=1)
    total = dot(grads, rows_ref[...], NT)
    for image, out in enumerate((g0, g1, g2, g3)):
        out[...] = total[image * seq : (image + 1) * seq].astype(out.dtype)


def context_gradient(places, grads, weights):
    _, seq, part = grads[0].shape
    rows, width = weights[0].shape
    block = rows // 4
    full = pl.BlockSpec((2, seq, part), lambda i, place: (0, 0, 0))
    by_row = pl.BlockSpec((block, width), lambda i, place: (i, 0))
    out = pl.BlockSpec((seq, block), lambda i, place: (0, i))
    return pl.pallas_call(
        context_gradient_body,
        grid_spec=pltpu.PrefetchScalarGridSpec(
            num_scalar_prefetch=1,
            grid=(4,),
            in_specs=[full] * 4
            + [by_row] * 3
            + [
                pl.BlockSpec((block, width), lambda i, place: (jnp.minimum(i, 1), 0)),
                pl.BlockSpec((block, width), lambda i, place: (jnp.maximum(i - 2, 0), 0)),
            ],
            out_specs=[out] * 4,
            scratch_shapes=[pltpu.VMEM((block, 2 * part), BF16)],
        ),
        out_shape=[
            jax.ShapeDtypeStruct((seq, rows), kind) for kind in (F32, BF16, F32, BF16)
        ],
        compiler_params=params(),
        cost_estimate=cost(16 * seq * part * rows, 20 * 2**20),
        name="context_gradient",
    )(places, *grads, *weights)


def weight_gradient_body(c0, c1, c2, c3, near, away, out_ref):
    context_t = jnp.concatenate([c[...] for c in (c0, c1, c2, c3)], axis=1)
    total = dot(context_t, four_images(near, away), (((1,), (0,)), ((), ())))
    for chip in range(16):
        out_ref[chip, 0] = total[chip * 24 : (chip + 1) * 24].astype(BF16)


def weight_gradient(contexts, near, away):
    rows, seq = contexts[0].shape
    features = near.shape[2]
    whole = pl.BlockSpec(near.shape, lambda i: (0, 0, 0))
    return pl.pallas_call(
        weight_gradient_body,
        grid=(4,),
        in_specs=[pl.BlockSpec((rows // 4, seq), lambda i: (i, 0))] * 4 + [whole] * 2,
        out_specs=pl.BlockSpec((16, 1, 24, features), lambda i: (0, i, 0, 0)),
        out_shape=jax.ShapeDtypeStruct((16, 4, 24, features), BF16),
        compiler_params=params(),
        cost_estimate=cost(8 * seq * features * rows, 8 * 2**20),
        name="weight_gradient",
    )(*contexts, near, away)


def sums_on_owners(terms, zh, c):
    sums = jnp.sum(terms.astype(F32), axis=0).astype(BF16)
    mine = lax.dynamic_index_in_dim(sums, zh, 0, False).astype(F32)
    for step in (1, 2, 3):
        away = lax.dynamic_index_in_dim(sums, (zh + step) % 4, 0, False)
        mine = mine + lax.ppermute(away, "zh", ring(4, step)).astype(F32)
    mine = mine.reshape(2, 12, -1)
    kept = jnp.where(c == 0, mine[0], mine[1])
    sent = jnp.where(c == 0, mine[1], mine[0])
    return kept, lax.ppermute(sent, "c", SWAP)


def per_device(queries, keys, values, grad_output, weight_codes, weight_scales):
    _, seq, total = queries.shape
    features = grad_output.shape[2]
    q, k, v = (a.reshape(seq, total) for a in (queries, keys, values))
    grad = grad_output.reshape(seq, features)
    zh, zl, xl, c, y = (lax.axis_index(name) for name in ("zh", "zl", "xl", "c", "y"))
    half = features // 2
    width = 384
    own_parity = zl.astype(jnp.int32).reshape(1)
    other_parity = 1 - own_parity

    places = jnp.stack([c * 4 + y, (1 - c) * 4 + y]).astype(jnp.int32)
    pieces = restore(places, weight_codes, weight_scales)
    arrived = lax.ppermute(pieces[1], "c", SWAP)
    pair = jnp.where(
        c == 0,
        jnp.concatenate([pieces[0], arrived], 0),
        jnp.concatenate([arrived, pieces[0]], 0),
    )
    from_behind = [lax.ppermute(pair, "zh", ring(4, step)) for step in (1, 2, 3)]
    turned = [pair, from_behind[2], from_behind[1], from_behind[0]]
    column = lax.dynamic_slice_in_dim(jnp.stack(turned + turned), (4 - zh) % 4, 4, 0)

    context_other = forward(other_parity, q, k, v, width)
    (context_other,) = after((context_other,), (column,))
    c2 = lax.ppermute(context_other, "zl", SWAP)
    context_own = forward(own_parity, q, k, v, width)
    c1 = lax.ppermute(context_own, "c", SWAP)

    beside = jnp.concatenate(
        [
            lax.ppermute(column[:2], ("xl", "xh"), x_ring(1)),
            lax.ppermute(column[2:], ("xl", "xh"), x_ring(-1)),
        ],
        0,
    )
    here = jnp.where(xl == 0, jnp.stack([column, beside], 1), jnp.stack([beside, column], 1))
    (here,) = after((here.reshape(-1, width),), (c1,))
    rows = here.shape[0]
    below = lax.ppermute(here, "y", ring(4, 1))
    above = lax.ppermute(here, "y", ring(4, -1))
    far_a = lax.ppermute(below[: rows // 2], "y", ring(4, 1))
    far_b = lax.ppermute(above[rows // 2 :], "y", ring(4, -1))
    (event,) = after((c2,), (here,))
    c3 = lax.ppermute(event, "c", SWAP)

    part = half // 2
    grads = []
    for index in range(2):
        own, partner = (
            lax.dynamic_slice_in_dim(grad, side * half + index * part, part, 1)
            for side in (c, 1 - c)
        )
        near = jnp.stack([own, lax.ppermute(partner, "c", SWAP)])
        (sent,) = after((near,), (column,) if index == 0 else (c2,))
        grads.append((near, lax.ppermute(sent, "zl", SWAP)))

    terms = []
    for near, away in grads:
        term = weight_gradient((context_own, c1, c2, c3), near, away)
        terms.append(lax.all_to_all(term, ("xl", "xh", "y"), 0, 0, tiled=True))

    places = jnp.stack([y, (y + 3) % 4, (y + 1) % 4, (y + 2) % 4]).astype(jnp.int32)
    g0, g1, g2, g3 = context_gradient(
        places, grads[0] + grads[1], (here, below, above, far_a, far_b)
    )
    r3 = lax.ppermute(g3, "c", SWAP)
    r1 = lax.ppermute(g1, "c", SWAP)
    g_other = lax.ppermute((g2 + r3.astype(F32)).astype(BF16), "zl", SWAP)
    first = backward(own_parity, q, k, v, (g0, r1), width)
    outs = backward(other_parity, q, k, v, (g_other,), width, first)

    (last,) = after((terms[1],), tuple(outs))
    kept, got = zip(*(sums_on_owners(term, zh, c) for term in (terms[0], last)))
    grad_weight = jnp.where(
        c == 0, jnp.concatenate(kept + got, 1), jnp.concatenate(got + kept, 1)
    )
    return tuple(out.reshape(1, seq, total) for out in outs) + (grad_weight,)


def solution(mesh):
    split = Mesh(mesh.devices.reshape(4, 2, 2, 2, 2, 4), AXES)
    image = P(AXES, None, None)
    return jax.shard_map(
        per_device,
        mesh=split,
        in_specs=(image, image, image, image, P(SHARD, None), P(SHARD, None)),
        out_specs=(image, image, image, P(AXES, None)),
        check_vma=False,
    )
```

```python
import functools

import jax
import jax.numpy as jnp
from jax import lax
from jax.experimental import pallas as pl
from jax.experimental.pallas import tpu as pltpu
from jax.sharding import Mesh
from jax.sharding import PartitionSpec as P

AXES = ("zh", "zl", "xl", "c", "xh", "y")
SHARD = ("zh", "zl", "xl", "c")
HD = 128
SCALE = HD**-0.5
F32 = jnp.float32
BF16 = jnp.bfloat16
SWAP = [(0, 1), (1, 0)]
NT = (((1,), (1,)), ((), ()))
TN = (((0,), (0,)), ((), ()))
VMEM_LIMIT = 50 * 2**20


def ring(count, step):
    return [(i, (i + step) % count) for i in range(count)]


def x_ring(step):
    def place(x):
        return (x % 2) * 2 + x // 2

    return [(place(x), place((x + step) % 4)) for x in range(4)]


def dot(a, b, dims):
    return lax.dot_general(a, b, dims, preferred_element_type=F32)


def params():
    return pltpu.CompilerParams(
        dimension_semantics=("arbitrary",), vmem_limit_bytes=VMEM_LIMIT
    )


def cost(flops, moved, exps=0):
    return pl.CostEstimate(flops=flops, bytes_accessed=moved, transcendentals=exps)


def softmax(q, k):
    scores = dot(q, k, NT) * SCALE
    exponent = jnp.exp(scores - jnp.max(scores, axis=1, keepdims=True))
    return exponent * (1.0 / jnp.sum(exponent, axis=1, keepdims=True))


def forward_body(pick, q_ref, k_ref, v_ref, out_ref, plain, sorted_rows):
    for head in range(q_ref.shape[1] // HD):
        cols = slice(head * HD, (head + 1) * HD)
        probs = softmax(q_ref[:, cols], k_ref[:, cols]).astype(BF16)
        plain[cols, :] = dot(v_ref[:, cols], probs, (((0,), (1,)), ((), ())))
    for xl in range(2):
        for xh in range(2):
            for y in range(4):
                for core in range(2):
                    old = xl * 192 + core * 96 + xh * 48 + y * 12
                    new = xl * 192 + xh * 96 + y * 24 + core * 12
                    sorted_rows[new : new + 12, :] = plain[old : old + 12, :]
    out_ref[...] = sorted_rows[...].astype(BF16)


def forward(parity, q, k, v, width):
    seq, total = q.shape
    blocks = total // width // 2
    spec = pl.BlockSpec((seq, width), lambda i, pick: (0, 2 * i + pick[0]))
    return pl.pallas_call(
        forward_body,
        grid_spec=pltpu.PrefetchScalarGridSpec(
            num_scalar_prefetch=1,
            grid=(blocks,),
            in_specs=[spec] * 3,
            out_specs=pl.BlockSpec((width, seq), lambda i, pick: (i, 0)),
            scratch_shapes=[pltpu.VMEM((width, seq), F32)] * 2,
        ),
        out_shape=jax.ShapeDtypeStruct((total // 2, seq), BF16),
        compiler_params=params(),
        cost_estimate=cost(2 * seq * seq * total, 2 * seq * total * 2, seq * seq * total // HD // 2),
        name="context_half",
    )(parity, q, k, v)


def backward_body(own, pick, q_ref, k_ref, v_ref, *refs):
    if own:
        g_ref, r_ref, gq_ref, gk_ref, gv_ref = refs
    else:
        g_ref, _, _, _, gq_ref, gk_ref, gv_ref = refs
    for head in range(q_ref.shape[1] // HD):
        cols = slice(head * HD, (head + 1) * HD)
        q, k, v = q_ref[:, cols], k_ref[:, cols], v_ref[:, cols]
        if own:
            g = (g_ref[:, cols] + r_ref[:, cols].astype(F32)).astype(BF16)
        else:
            g = g_ref[:, cols]
        probs = softmax(q, k)
        gv_ref[:, cols] = dot(probs.astype(BF16), g, TN).astype(BF16)
        dprobs = dot(g, v, NT)
        delta = jnp.sum(probs * dprobs, axis=1, keepdims=True)
        dscores = (probs * (dprobs - delta) * SCALE).astype(BF16)
        gq_ref[:, cols] = dot(dscores, k, (((1,), (0,)), ((), ()))).astype(BF16)
        gk_ref[:, cols] = dot(dscores, q, TN).astype(BF16)


def backward(parity, q, k, v, grads, width, before=None):
    seq, total = q.shape
    blocks = total // width // 2
    spec = pl.BlockSpec((seq, width), lambda i, pick: (0, 2 * i + pick[0]))
    half = pl.BlockSpec((seq, width), lambda i, pick: (0, i))
    whole = jax.ShapeDtypeStruct((seq, total), BF16)
    extra = [] if before is None else list(before)
    return pl.pallas_call(
        functools.partial(backward_body, before is None),
        grid_spec=pltpu.PrefetchScalarGridSpec(
            num_scalar_prefetch=1,
            grid=(blocks,),
            in_specs=[spec] * 3
            + [half] * len(grads)
            + [pl.BlockSpec(memory_space=pl.ANY)] * len(extra),
            out_specs=[spec] * 3,
        ),
        out_shape=[whole] * 3,
        input_output_aliases={} if before is None else {5: 0, 6: 1, 7: 2},
        compiler_params=params(),
        cost_estimate=cost(5 * seq * seq * total, 7 * seq * total, seq * seq * total // HD // 2),
        name="attention_gradients",
    )(parity, q, k, v, *grads, *extra)


def after(values, events):
    return lax.optimization_barrier((values, events))[0]


def restore_body(codes_ref, scales_ref, near_ref, away_ref):
    core, y = lax.axis_index("c"), lax.axis_index("y")
    blocks = scales_ref.shape[0]
    width = near_ref.shape[1]
    for side, out in ((core, near_ref), (1 - core, away_ref)):
        first = (side * 4 + y) * (width // 128)
        for tile in range(width // 128):
            column = first + tile
            codes = codes_ref[:, pl.ds(pl.multiple_of(column * 128, 128), 128)].astype(F32)
            lane = lax.broadcasted_iota(jnp.int32, (blocks, 128), 0)
            chosen = jnp.where(lane == column // 2, 1.0, 0.0)
            scale = lax.dot_general(
                scales_ref[...],
                chosen,
                TN,
                precision=lax.Precision.HIGHEST,
                preferred_element_type=F32,
            )
            out[:, tile * 128 : (tile + 1) * 128] = (codes * scale).astype(BF16)


def restore(codes, scales):
    rows = codes.shape[0]
    return pl.pallas_call(
        restore_body,
        out_shape=[jax.ShapeDtypeStruct((rows, 384), BF16)] * 2,
        cost_estimate=cost(rows * 768, rows * 3072),
        name="weight_pieces",
    )(codes, scales)


def by_zh_body(own_ref, b1, b2, b3, low_ref, high_ref):
    zh = lax.axis_index("zh")
    for step, piece in enumerate((own_ref, b1, b2, b3)):
        place = lax.rem(zh - step + 4, 4)

        @pl.when(place < 2)
        def _():
            low_ref[place] = piece[...]

        @pl.when(place >= 2)
        def _():
            high_ref[place - 2] = piece[...]


def by_zh(own, pieces):
    return pl.pallas_call(
        by_zh_body,
        out_shape=[jax.ShapeDtypeStruct((2, *own.shape), BF16)] * 2,
        cost_estimate=cost(own.size, own.size * 16),
        name="weight_by_zh",
    )(own, *pieces)


def by_xl_body(low, high, beside_low, beside_high, low_ref, high_ref):
    xl = lax.axis_index("xl")
    for mine, beside, out in ((low, beside_low, low_ref), (high, beside_high, high_ref)):
        for place in range(2):
            out[place, xl] = mine[place]
            out[place, 1 - xl] = beside[place]


def by_xl(low, high, beside_low, beside_high):
    shape = (2, 2, *low.shape[1:])
    return pl.pallas_call(
        by_xl_body,
        out_shape=[jax.ShapeDtypeStruct(shape, BF16)] * 2,
        cost_estimate=cost(low.size, low.size * 16),
        name="weight_by_xl",
    )(low, high, beside_low, beside_high)


def four_images(near, away):
    return jnp.concatenate([near[0], near[1], away[0], away[1]], axis=0)


def context_gradient_body(place, a0, a1, b0, b1, *refs):
    lows, highs, outs, rows_ref = refs[:4], refs[4:8], refs[8:12], refs[12]
    seq = a0.shape[1]

    def gather(weights):
        width = weights[0].shape[1]
        for part, weight in enumerate(weights):
            cols = pl.ds(pl.multiple_of(place[part] * width, 128), width)
            rows_ref[:, cols] = weight[...]

    pl.when(pl.program_id(0) < 2)(functools.partial(gather, lows))
    pl.when(pl.program_id(0) >= 2)(functools.partial(gather, highs))
    grads = jnp.concatenate([four_images(a0, a1), four_images(b0, b1)], axis=1)
    total = dot(grads, rows_ref[...], NT)
    for image, out in enumerate(outs):
        out[...] = total[image * seq : (image + 1) * seq].astype(out.dtype)


def context_gradient(places, grads, lows, highs):
    _, seq, part = grads[0].shape
    block, width = lows[0].shape[0] // 2, lows[0].shape[1]
    rows = 4 * block
    full = pl.BlockSpec((2, seq, part), lambda i, place: (0, 0, 0))
    low = pl.BlockSpec((block, width), lambda i, place: (jnp.minimum(i, 1), 0))
    high = pl.BlockSpec((block, width), lambda i, place: (jnp.maximum(i - 2, 0), 0))
    out = pl.BlockSpec((seq, block), lambda i, place: (0, i))
    return pl.pallas_call(
        context_gradient_body,
        grid_spec=pltpu.PrefetchScalarGridSpec(
            num_scalar_prefetch=1,
            grid=(4,),
            in_specs=[full] * 4 + [low] * 4 + [high] * 4,
            out_specs=[out] * 4,
            scratch_shapes=[pltpu.VMEM((block, 2 * part), BF16)],
        ),
        out_shape=[
            jax.ShapeDtypeStruct((seq, rows), kind) for kind in (F32, BF16, F32, BF16)
        ],
        compiler_params=params(),
        cost_estimate=cost(16 * seq * part * rows, 20 * 2**20),
        name="context_gradient",
    )(places, *grads, *lows, *highs)


def weight_gradient_body(c0, c1, c2, c3, near, away, out_ref):
    context_t = jnp.concatenate([c[...] for c in (c0, c1, c2, c3)], axis=1)
    total = dot(context_t, four_images(near, away), (((1,), (0,)), ((), ())))
    for chip in range(16):
        out_ref[chip, 0] = total[chip * 24 : (chip + 1) * 24].astype(BF16)


def weight_gradient(contexts, near, away):
    rows, seq = contexts[0].shape
    features = near.shape[2]
    whole = pl.BlockSpec(near.shape, lambda i: (0, 0, 0))
    return pl.pallas_call(
        weight_gradient_body,
        grid=(4,),
        in_specs=[pl.BlockSpec((rows // 4, seq), lambda i: (i, 0))] * 4 + [whole] * 2,
        out_specs=pl.BlockSpec((16, 1, 24, features), lambda i: (0, i, 0, 0)),
        out_shape=jax.ShapeDtypeStruct((16, 4, 24, features), BF16),
        compiler_params=params(),
        cost_estimate=cost(8 * seq * features * rows, 8 * 2**20),
        name="weight_gradient",
    )(*contexts, near, away)


def sums_on_owners(terms, zh, c):
    sums = jnp.sum(terms.astype(F32), axis=0).astype(BF16)
    mine = lax.dynamic_index_in_dim(sums, zh, 0, False).astype(F32)
    for step in (1, 2, 3):
        away = lax.dynamic_index_in_dim(sums, (zh + step) % 4, 0, False)
        mine = mine + lax.ppermute(away, "zh", ring(4, step)).astype(F32)
    mine = mine.reshape(2, 12, -1)
    kept = jnp.where(c == 0, mine[0], mine[1])
    sent = jnp.where(c == 0, mine[1], mine[0])
    return kept, lax.ppermute(sent, "c", SWAP)


def per_device(queries, keys, values, grad_output, weight_codes, weight_scales):
    _, seq, total = queries.shape
    features = grad_output.shape[2]
    q, k, v = (a.reshape(seq, total) for a in (queries, keys, values))
    grad = grad_output.reshape(seq, features)
    zh, zl, xl, c, y = (lax.axis_index(name) for name in ("zh", "zl", "xl", "c", "y"))
    half = features // 2
    width = 384
    own_parity = zl.astype(jnp.int32).reshape(1)
    other_parity = 1 - own_parity

    piece, sent = restore(weight_codes, weight_scales.T)
    arrived = lax.ppermute(sent, "c", SWAP)
    pair = jnp.where(
        c == 0, jnp.concatenate([piece, arrived], 0), jnp.concatenate([arrived, piece], 0)
    )
    behind = [lax.ppermute(pair, "zh", ring(4, step)) for step in (1, 2, 3)]
    low, high = by_zh(pair, behind)
    start = low
    beside_low = lax.ppermute(low, ("xl", "xh"), x_ring(1))
    beside_high = lax.ppermute(high, ("xl", "xh"), x_ring(-1))

    q, k = after((q, k), (behind[0],))
    context_other = forward(other_parity, q, k, v, width)
    (context_other,) = after((context_other,), (low,))
    c2 = lax.ppermute(context_other, "zl", SWAP)
    context_own = forward(own_parity, q, k, v, width)
    c1 = lax.ppermute(context_own, "c", SWAP)

    low, high = by_xl(low, high, beside_low, beside_high)
    lows, highs = ([piece.reshape(-1, width)] for piece in (low, high))
    for step in (1, -1):
        lows.append(lax.ppermute(lows[0], "y", ring(4, step)))
        highs.append(lax.ppermute(highs[0], "y", ring(4, step)))
    lows.append(lax.ppermute(lows[1], "y", ring(4, 1)))
    highs.append(lax.ppermute(highs[2], "y", ring(4, -1)))
    (event,) = after((c2,), (lows[1], highs[2]))
    c3 = lax.ppermute(event, "c", SWAP)

    part = half // 2
    grads = []
    for index in range(2):
        own, partner = (
            lax.dynamic_slice_in_dim(grad, side * half + index * part, part, 1)
            for side in (c, 1 - c)
        )
        near = jnp.stack([own, lax.ppermute(partner, "c", SWAP)])
        (sent,) = after((near,), (start,) if index == 0 else (c2,))
        grads.append((near, lax.ppermute(sent, "zl", SWAP)))

    (c1,) = after((c1,), (lows[2], highs[1]))
    terms = []
    for near, away in grads:
        term = weight_gradient((context_own, c1, c2, c3), near, away)
        (term,) = after((term,), (lows[3], highs[3]))
        terms.append(lax.all_to_all(term, ("xl", "xh", "y"), 0, 0, tiled=True))

    places = jnp.stack([y, (y + 3) % 4, (y + 1) % 4, (y + 2) % 4]).astype(jnp.int32)
    (near,) = after(grads[0][:1], (term,))
    g0, g1, g2, g3 = context_gradient(
        places, (near, grads[0][1]) + grads[1], lows, highs
    )
    r3 = lax.ppermute(g3, "c", SWAP)
    r1 = lax.ppermute(g1, "c", SWAP)
    g_other = lax.ppermute((g2 + r3.astype(F32)).astype(BF16), "zl", SWAP)
    first = backward(own_parity, q, k, v, (g0, r1), width)
    outs = backward(other_parity, q, k, v, (g_other,), width, first)

    (last,) = after((terms[1],), tuple(outs))
    kept, got = zip(*(sums_on_owners(term, zh, c) for term in (terms[0], last)))
    grad_weight = jnp.where(
        c == 0, jnp.concatenate(kept + got, 1), jnp.concatenate(got + kept, 1)
    )
    return tuple(out.reshape(1, seq, total) for out in outs) + (grad_weight,)


def solution(mesh):
    split = Mesh(mesh.devices.reshape(4, 2, 2, 2, 2, 4), AXES)
    image = P(AXES, None, None)
    return jax.shard_map(
        per_device,
        mesh=split,
        in_specs=(image, image, image, image, P(SHARD, None), P(SHARD, None)),
        out_specs=(image, image, image, P(AXES, None)),
        check_vma=False,
    )
```

```python
import functools

import jax
import jax.numpy as jnp
from jax import lax
from jax.experimental import pallas as pl
from jax.experimental.pallas import tpu as pltpu
from jax.sharding import Mesh
from jax.sharding import PartitionSpec as P

AXES = ("zh", "zl", "xl", "c", "xh", "y")
SHARD = ("zh", "zl", "xl", "c")
HD = 128
SCALE = HD**-0.5
F32 = jnp.float32
BF16 = jnp.bfloat16
SWAP = [(0, 1), (1, 0)]
NT = (((1,), (1,)), ((), ()))
TN = (((0,), (0,)), ((), ()))
VMEM_LIMIT = 60 * 2**20


def ring(count, step):
    return [(i, (i + step) % count) for i in range(count)]


def x_ring(step):
    def place(x):
        return (x % 2) * 2 + x // 2

    return [(place(x), place((x + step) % 4)) for x in range(4)]


def dot(a, b, dims):
    return lax.dot_general(a, b, dims, preferred_element_type=F32)


def params():
    return pltpu.CompilerParams(
        dimension_semantics=("arbitrary",), vmem_limit_bytes=VMEM_LIMIT
    )


def cost(flops, moved, exps=0):
    return pl.CostEstimate(flops=flops, bytes_accessed=moved, transcendentals=exps)


def softmax(q, k):
    scores = dot(q, k, NT) * SCALE
    exponent = jnp.exp(scores - jnp.max(scores, axis=1, keepdims=True))
    return exponent * (1.0 / jnp.sum(exponent, axis=1, keepdims=True))


def forward_body(pick, q_ref, k_ref, v_ref, out_ref, plain, sorted_rows):
    for head in range(q_ref.shape[1] // HD):
        cols = slice(head * HD, (head + 1) * HD)
        probs = softmax(q_ref[:, cols], k_ref[:, cols]).astype(BF16)
        plain[cols, :] = dot(v_ref[:, cols], probs, (((0,), (1,)), ((), ())))
    for xl in range(2):
        for xh in range(2):
            for y in range(4):
                for core in range(2):
                    old = xl * 192 + core * 96 + xh * 48 + y * 12
                    new = xl * 192 + xh * 96 + y * 24 + core * 12
                    sorted_rows[new : new + 12, :] = plain[old : old + 12, :]
    out_ref[...] = sorted_rows[...].astype(BF16)


def forward(parity, q, k, v, width):
    seq, total = q.shape
    blocks = total // width // 2
    spec = pl.BlockSpec((seq, width), lambda i, pick: (0, 2 * i + pick[0]))
    return pl.pallas_call(
        forward_body,
        grid_spec=pltpu.PrefetchScalarGridSpec(
            num_scalar_prefetch=1,
            grid=(blocks,),
            in_specs=[spec] * 3,
            out_specs=pl.BlockSpec((width, seq), lambda i, pick: (i, 0)),
            scratch_shapes=[pltpu.VMEM((width, seq), F32)] * 2,
        ),
        out_shape=jax.ShapeDtypeStruct((total // 2, seq), BF16),
        compiler_params=params(),
        cost_estimate=cost(2 * seq * seq * total, 2 * seq * total * 2, seq * seq * total // HD // 2),
        name="context_half",
    )(parity, q, k, v)


def backward_body(own, pick, q_ref, k_ref, v_ref, *refs):
    if own:
        g_ref, r_ref, gq_ref, gk_ref, gv_ref = refs
    else:
        g_ref, _, _, _, gq_ref, gk_ref, gv_ref = refs
    for head in range(q_ref.shape[1] // HD):
        cols = slice(head * HD, (head + 1) * HD)
        q, k, v = q_ref[:, cols], k_ref[:, cols], v_ref[:, cols]
        if own:
            g = (g_ref[:, cols] + r_ref[:, cols].astype(F32)).astype(BF16)
        else:
            g = g_ref[:, cols]
        probs = softmax(q, k)
        gv_ref[:, cols] = dot(probs.astype(BF16), g, TN).astype(BF16)
        dprobs = dot(g, v, NT)
        delta = jnp.sum(probs * dprobs, axis=1, keepdims=True)
        dscores = (probs * (dprobs - delta) * SCALE).astype(BF16)
        gq_ref[:, cols] = dot(dscores, k, (((1,), (0,)), ((), ()))).astype(BF16)
        gk_ref[:, cols] = dot(dscores, q, TN).astype(BF16)


def backward(parity, q, k, v, grads, width, before=None):
    seq, total = q.shape
    blocks = total // width // 2
    spec = pl.BlockSpec((seq, width), lambda i, pick: (0, 2 * i + pick[0]))
    half = pl.BlockSpec((seq, width), lambda i, pick: (0, i))
    whole = jax.ShapeDtypeStruct((seq, total), BF16)
    extra = [] if before is None else list(before)
    return pl.pallas_call(
        functools.partial(backward_body, before is None),
        grid_spec=pltpu.PrefetchScalarGridSpec(
            num_scalar_prefetch=1,
            grid=(blocks,),
            in_specs=[spec] * 3
            + [half] * len(grads)
            + [pl.BlockSpec(memory_space=pl.ANY)] * len(extra),
            out_specs=[spec] * 3,
        ),
        out_shape=[whole] * 3,
        input_output_aliases={} if before is None else {5: 0, 6: 1, 7: 2},
        compiler_params=params(),
        cost_estimate=cost(5 * seq * seq * total, 7 * seq * total, seq * seq * total // HD // 2),
        name="attention_gradients",
    )(parity, q, k, v, *grads, *extra)


def after(values, events):
    return lax.optimization_barrier((values, events))[0]


def restore_body(codes_ref, scales_ref, near_ref, away_ref):
    core, y = lax.axis_index("c"), lax.axis_index("y")
    blocks = scales_ref.shape[0]
    width = near_ref.shape[1]
    for side, out in ((core, near_ref), (1 - core, away_ref)):
        first = (side * 4 + y) * (width // 128)
        for tile in range(width // 128):
            column = first + tile
            codes = codes_ref[:, pl.ds(pl.multiple_of(column * 128, 128), 128)].astype(F32)
            lane = lax.broadcasted_iota(jnp.int32, (blocks, 128), 0)
            chosen = jnp.where(lane == column // 2, 1.0, 0.0)
            scale = lax.dot_general(
                scales_ref[...],
                chosen,
                TN,
                precision=lax.Precision.HIGHEST,
                preferred_element_type=F32,
            )
            out[:, tile * 128 : (tile + 1) * 128] = (codes * scale).astype(BF16)


def restore(codes, scales):
    rows = codes.shape[0]
    return pl.pallas_call(
        restore_body,
        out_shape=[jax.ShapeDtypeStruct((rows, 384), BF16)] * 2,
        compiler_params=pltpu.CompilerParams(vmem_limit_bytes=VMEM_LIMIT),
        cost_estimate=cost(rows * 768, rows * 3072),
        name="weight_pieces",
    )(codes, scales)


def by_zh_body(own_ref, b1, b2, b3, low_ref, high_ref):
    zh = lax.axis_index("zh")
    for step, piece in enumerate((own_ref, b1, b2, b3)):
        place = lax.rem(zh - step + 4, 4)

        @pl.when(place < 2)
        def _():
            low_ref[place] = piece[...]

        @pl.when(place >= 2)
        def _():
            high_ref[place - 2] = piece[...]


def by_zh(own, pieces):
    return pl.pallas_call(
        by_zh_body,
        out_shape=[jax.ShapeDtypeStruct((2, *own.shape), BF16)] * 2,
        compiler_params=pltpu.CompilerParams(vmem_limit_bytes=VMEM_LIMIT),
        cost_estimate=cost(own.size, own.size * 16),
        name="weight_by_zh",
    )(own, *pieces)


def by_xl_body(low, high, beside_low, beside_high, low_ref, high_ref):
    xl = lax.axis_index("xl")
    for mine, beside, out in ((low, beside_low, low_ref), (high, beside_high, high_ref)):
        for place in range(2):
            out[place, xl] = mine[place]
            out[place, 1 - xl] = beside[place]


def by_xl(low, high, beside_low, beside_high):
    shape = (2, 2, *low.shape[1:])
    return pl.pallas_call(
        by_xl_body,
        out_shape=[jax.ShapeDtypeStruct(shape, BF16)] * 2,
        compiler_params=pltpu.CompilerParams(vmem_limit_bytes=VMEM_LIMIT),
        cost_estimate=cost(low.size, low.size * 16),
        name="weight_by_xl",
    )(low, high, beside_low, beside_high)


def four_images(near, away):
    return jnp.concatenate([near[0], near[1], away[0], away[1]], axis=0)


def context_gradient_body(place, a0, a1, b0, b1, *refs):
    lows, highs, outs, rows_ref = refs[:4], refs[4:8], refs[8:12], refs[12]
    seq = a0.shape[1]

    def gather(weights):
        width = weights[0].shape[1]
        for part, weight in enumerate(weights):
            cols = pl.ds(pl.multiple_of(place[part] * width, 128), width)
            rows_ref[:, cols] = weight[...]

    pl.when(pl.program_id(0) < 2)(functools.partial(gather, lows))
    pl.when(pl.program_id(0) >= 2)(functools.partial(gather, highs))
    grads = jnp.concatenate([four_images(a0, a1), four_images(b0, b1)], axis=1)
    total = dot(grads, rows_ref[...], NT)
    for image, out in enumerate(outs):
        out[...] = total[image * seq : (image + 1) * seq].astype(out.dtype)


def context_gradient(places, grads, lows, highs):
    _, seq, part = grads[0].shape
    block, width = lows[0].shape[0] // 2, lows[0].shape[1]
    rows = 4 * block
    full = pl.BlockSpec((2, seq, part), lambda i, place: (0, 0, 0))
    low = pl.BlockSpec((block, width), lambda i, place: (jnp.minimum(i, 1), 0))
    high = pl.BlockSpec((block, width), lambda i, place: (jnp.maximum(i - 2, 0), 0))
    out = pl.BlockSpec((seq, block), lambda i, place: (0, i))
    return pl.pallas_call(
        context_gradient_body,
        grid_spec=pltpu.PrefetchScalarGridSpec(
            num_scalar_prefetch=1,
            grid=(4,),
            in_specs=[full] * 4 + [low] * 4 + [high] * 4,
            out_specs=[out] * 4,
            scratch_shapes=[pltpu.VMEM((block, 2 * part), BF16)],
        ),
        out_shape=[
            jax.ShapeDtypeStruct((seq, rows), kind) for kind in (F32, BF16, F32, BF16)
        ],
        compiler_params=params(),
        cost_estimate=cost(16 * seq * part * rows, 20 * 2**20),
        name="context_gradient",
    )(places, *grads, *lows, *highs)


def weight_gradient_body(c0, c1, c2, c3, near, away, out_ref):
    context_t = jnp.concatenate([c[...] for c in (c0, c1, c2, c3)], axis=1)
    total = dot(context_t, four_images(near, away), (((1,), (0,)), ((), ())))
    for chip in range(16):
        out_ref[chip, 0] = total[chip * 24 : (chip + 1) * 24].astype(BF16)


def weight_gradient(contexts, near, away):
    rows, seq = contexts[0].shape
    features = near.shape[2]
    whole = pl.BlockSpec(near.shape, lambda i: (0, 0, 0))
    return pl.pallas_call(
        weight_gradient_body,
        grid=(4,),
        in_specs=[pl.BlockSpec((rows // 4, seq), lambda i: (i, 0))] * 4 + [whole] * 2,
        out_specs=pl.BlockSpec((16, 1, 24, features), lambda i: (0, i, 0, 0)),
        out_shape=jax.ShapeDtypeStruct((16, 4, 24, features), BF16),
        compiler_params=params(),
        cost_estimate=cost(8 * seq * features * rows, 8 * 2**20),
        name="weight_gradient",
    )(*contexts, near, away)


def sums_on_owners(terms, zh, c):
    sums = jnp.sum(terms.astype(F32), axis=0).astype(BF16)
    mine = lax.dynamic_index_in_dim(sums, zh, 0, False).astype(F32)
    for step in (1, 2, 3):
        away = lax.dynamic_index_in_dim(sums, (zh + step) % 4, 0, False)
        mine = mine + lax.ppermute(away, "zh", ring(4, step)).astype(F32)
    mine = mine.reshape(2, 12, -1)
    kept = jnp.where(c == 0, mine[0], mine[1])
    sent = jnp.where(c == 0, mine[1], mine[0])
    return kept, lax.ppermute(sent, "c", SWAP)


def per_device(queries, keys, values, grad_output, weight_codes, weight_scales):
    _, seq, total = queries.shape
    features = grad_output.shape[2]
    q, k, v = (a.reshape(seq, total) for a in (queries, keys, values))
    grad = grad_output.reshape(seq, features)
    zh, zl, xl, c, y = (lax.axis_index(name) for name in ("zh", "zl", "xl", "c", "y"))
    half = features // 2
    width = 384
    own_parity = zl.astype(jnp.int32).reshape(1)
    other_parity = 1 - own_parity

    piece, sent = restore(weight_codes, weight_scales.T)
    arrived = lax.ppermute(sent, "c", SWAP)
    pair = jnp.where(
        c == 0, jnp.concatenate([piece, arrived], 0), jnp.concatenate([arrived, piece], 0)
    )
    behind = [lax.ppermute(pair, "zh", ring(4, step)) for step in (1, 2, 3)]
    (late_parity,) = after((other_parity,), (behind[0],))
    context_other = forward(late_parity, q, k, v, width)
    (pair,) = after((pair,), (context_other,))
    low, high = by_zh(pair, behind)
    start = low
    beside_low = lax.ppermute(low, ("xl", "xh"), x_ring(1))
    beside_high = lax.ppermute(high, ("xl", "xh"), x_ring(-1))

    (context_other,) = after((context_other,), (behind[1], behind[2]))
    c2 = lax.ppermute(context_other, "zl", SWAP)
    context_own = forward(own_parity, q, k, v, width)
    c1 = lax.ppermute(context_own, "c", SWAP)

    part = half // 2
    nears, grads = [], []
    for index in range(2):
        own, partner = (
            lax.dynamic_slice_in_dim(grad, side * half + index * part, part, 1)
            for side in (c, 1 - c)
        )
        nears.append(jnp.stack([own, lax.ppermute(partner, "c", SWAP)]))
        (sent,) = after(nears[-1:], (grads[0][1] if index else start,))
        grads.append((nears[-1], lax.ppermute(sent, "zl", SWAP)))

    low, high = by_xl(low, high, beside_low, beside_high)
    lows, highs = ([piece.reshape(-1, width)] for piece in (low, high))
    for step in (1, -1):
        lows.append(lax.ppermute(lows[0], "y", ring(4, step)))
        highs.append(lax.ppermute(highs[0], "y", ring(4, step)))
    lows.append(lax.ppermute(lows[1], "y", ring(4, 1)))
    highs.append(lax.ppermute(highs[2], "y", ring(4, -1)))
    (event,) = after((c2,), (lows[1], highs[2], nears[1]))
    c3 = lax.ppermute(event, "c", SWAP)

    (c1,) = after((c1,), (lows[2], highs[1]))
    terms = []
    for near, away in grads:
        term = weight_gradient((context_own, c1, c2, c3), near, away)
        (term,) = after((term,), (lows[3], highs[3]))
        terms.append(lax.all_to_all(term, ("xl", "xh", "y"), 0, 0, tiled=True))

    places = jnp.stack([y, (y + 3) % 4, (y + 1) % 4, (y + 2) % 4]).astype(jnp.int32)
    g0, g1, g2, g3 = context_gradient(places, grads[0] + grads[1], lows, highs)
    r3 = lax.ppermute(g3, "c", SWAP)
    r1 = lax.ppermute(g1, "c", SWAP)
    g_other = lax.ppermute((g2 + r3.astype(F32)).astype(BF16), "zl", SWAP)
    first = backward(own_parity, q, k, v, (g0, r1), width)

    kept_a, got_a = sums_on_owners(terms[0], zh, c)
    (g_other,) = after((g_other,), (kept_a, got_a))
    outs = backward(other_parity, q, k, v, (g_other,), width, first)
    (last,) = after((terms[1],), tuple(outs))
    kept_b, got_b = sums_on_owners(last, zh, c)
    kept, got = (kept_a, kept_b), (got_a, got_b)
    grad_weight = jnp.where(
        c == 0, jnp.concatenate(kept + got, 1), jnp.concatenate(got + kept, 1)
    )
    return tuple(out.reshape(1, seq, total) for out in outs) + (grad_weight,)


def solution(mesh):
    split = Mesh(mesh.devices.reshape(4, 2, 2, 2, 2, 4), AXES)
    image = P(AXES, None, None)
    return jax.shard_map(
        per_device,
        mesh=split,
        in_specs=(image, image, image, image, P(SHARD, None), P(SHARD, None)),
        out_specs=(image, image, image, P(AXES, None)),
        check_vma=False,
    )
```

```python
import functools

import jax
import jax.numpy as jnp
from jax import lax
from jax.experimental import pallas as pl
from jax.experimental.pallas import tpu as pltpu
from jax.sharding import Mesh
from jax.sharding import PartitionSpec as P

AXES = ("zh", "zl", "xl", "c", "xh", "y")
SHARD = ("zh", "zl", "xl", "c")
HD = 128
SCALE = HD**-0.5
F32 = jnp.float32
BF16 = jnp.bfloat16
SWAP = [(0, 1), (1, 0)]
NT = (((1,), (1,)), ((), ()))
TN = (((0,), (0,)), ((), ()))
VMEM_LIMIT = 60 * 2**20


def ring(count, step):
    return [(i, (i + step) % count) for i in range(count)]


def x_ring(step):
    def place(x):
        return (x % 2) * 2 + x // 2

    return [(place(x), place((x + step) % 4)) for x in range(4)]


def dot(a, b, dims):
    return lax.dot_general(a, b, dims, preferred_element_type=F32)


def params():
    return pltpu.CompilerParams(
        dimension_semantics=("arbitrary",), vmem_limit_bytes=VMEM_LIMIT
    )


def cost(flops, moved, exps=0):
    return pl.CostEstimate(flops=flops, bytes_accessed=moved, transcendentals=exps)


def softmax(q, k):
    scores = dot(q, k, NT) * SCALE
    exponent = jnp.exp(scores - jnp.max(scores, axis=1, keepdims=True))
    return exponent * (1.0 / jnp.sum(exponent, axis=1, keepdims=True))


def forward_body(pick, q_ref, k_ref, v_ref, out_ref, plain, sorted_rows):
    for head in range(q_ref.shape[1] // HD):
        cols = slice(head * HD, (head + 1) * HD)
        probs = softmax(q_ref[:, cols], k_ref[:, cols]).astype(BF16)
        plain[cols, :] = dot(v_ref[:, cols], probs, (((0,), (1,)), ((), ())))
    for xl in range(2):
        for xh in range(2):
            for y in range(4):
                for core in range(2):
                    old = xl * 192 + core * 96 + xh * 48 + y * 12
                    new = xl * 192 + xh * 96 + y * 24 + core * 12
                    sorted_rows[new : new + 12, :] = plain[old : old + 12, :]
    out_ref[...] = sorted_rows[...].astype(BF16)


def forward(parity, q, k, v, width):
    seq, total = q.shape
    blocks = total // width // 2
    spec = pl.BlockSpec((seq, width), lambda i, pick: (0, 2 * i + pick[0]))
    return pl.pallas_call(
        forward_body,
        grid_spec=pltpu.PrefetchScalarGridSpec(
            num_scalar_prefetch=1,
            grid=(blocks,),
            in_specs=[spec] * 3,
            out_specs=pl.BlockSpec((width, seq), lambda i, pick: (i, 0)),
            scratch_shapes=[pltpu.VMEM((width, seq), F32)] * 2,
        ),
        out_shape=jax.ShapeDtypeStruct((total // 2, seq), BF16),
        compiler_params=params(),
        cost_estimate=cost(2 * seq * seq * total, 2 * seq * total * 2, seq * seq * total // HD // 2),
        name="context_half",
    )(parity, q, k, v)


def backward_body(own, pick, q_ref, k_ref, v_ref, *refs):
    if own:
        g_ref, r_ref, gq_ref, gk_ref, gv_ref = refs
    else:
        g_ref, _, _, _, gq_ref, gk_ref, gv_ref = refs
    for head in range(q_ref.shape[1] // HD):
        cols = slice(head * HD, (head + 1) * HD)
        q, k, v = q_ref[:, cols], k_ref[:, cols], v_ref[:, cols]
        if own:
            g = (g_ref[:, cols] + r_ref[:, cols].astype(F32)).astype(BF16)
        else:
            g = g_ref[:, cols]
        probs = softmax(q, k)
        gv_ref[:, cols] = dot(probs.astype(BF16), g, TN).astype(BF16)
        dprobs = dot(g, v, NT)
        delta = jnp.sum(probs * dprobs, axis=1, keepdims=True)
        dscores = (probs * (dprobs - delta) * SCALE).astype(BF16)
        gq_ref[:, cols] = dot(dscores, k, (((1,), (0,)), ((), ()))).astype(BF16)
        gk_ref[:, cols] = dot(dscores, q, TN).astype(BF16)


def backward(parity, q, k, v, grads, width, before=None):
    seq, total = q.shape
    blocks = total // width // 2
    spec = pl.BlockSpec((seq, width), lambda i, pick: (0, 2 * i + pick[0]))
    half = pl.BlockSpec((seq, width), lambda i, pick: (0, i))
    whole = jax.ShapeDtypeStruct((seq, total), BF16)
    extra = [] if before is None else list(before)
    return pl.pallas_call(
        functools.partial(backward_body, before is None),
        grid_spec=pltpu.PrefetchScalarGridSpec(
            num_scalar_prefetch=1,
            grid=(blocks,),
            in_specs=[spec] * 3
            + [half] * len(grads)
            + [pl.BlockSpec(memory_space=pl.ANY)] * len(extra),
            out_specs=[spec] * 3,
        ),
        out_shape=[whole] * 3,
        input_output_aliases={} if before is None else {5: 0, 6: 1, 7: 2},
        compiler_params=params(),
        cost_estimate=cost(5 * seq * seq * total, 7 * seq * total, seq * seq * total // HD // 2),
        name="attention_gradients",
    )(parity, q, k, v, *grads, *extra)


def after(values, events):
    return lax.optimization_barrier((values, events))[0]


def restore_body(codes_ref, scales_ref, near_ref, away_ref):
    core, y = lax.axis_index("c"), lax.axis_index("y")
    blocks = scales_ref.shape[0]
    width = near_ref.shape[1]
    for side, out in ((core, near_ref), (1 - core, away_ref)):
        first = (side * 4 + y) * (width // 128)
        for tile in range(width // 128):
            column = first + tile
            codes = codes_ref[:, pl.ds(pl.multiple_of(column * 128, 128), 128)].astype(F32)
            lane = lax.broadcasted_iota(jnp.int32, (blocks, 128), 0)
            chosen = jnp.where(lane == column // 2, 1.0, 0.0)
            scale = lax.dot_general(
                scales_ref[...],
                chosen,
                TN,
                precision=lax.Precision.HIGHEST,
                preferred_element_type=F32,
            )
            out[:, tile * 128 : (tile + 1) * 128] = (codes * scale).astype(BF16)


def restore(codes, scales):
    rows = codes.shape[0]
    return pl.pallas_call(
        restore_body,
        out_shape=[jax.ShapeDtypeStruct((rows, 384), BF16)] * 2,
        compiler_params=pltpu.CompilerParams(vmem_limit_bytes=VMEM_LIMIT),
        cost_estimate=cost(rows * 768, rows * 3072),
        name="weight_pieces",
    )(codes, scales)


def by_zh_body(own_ref, b1, b2, b3, low_ref, high_ref):
    zh = lax.axis_index("zh")
    for step, piece in enumerate((own_ref, b1, b2, b3)):
        place = lax.rem(zh - step + 4, 4)

        @pl.when(place < 2)
        def _():
            low_ref[place] = piece[...]

        @pl.when(place >= 2)
        def _():
            high_ref[place - 2] = piece[...]


def by_zh(own, pieces):
    return pl.pallas_call(
        by_zh_body,
        out_shape=[jax.ShapeDtypeStruct((2, *own.shape), BF16)] * 2,
        compiler_params=pltpu.CompilerParams(vmem_limit_bytes=VMEM_LIMIT),
        cost_estimate=cost(own.size, own.size * 16),
        name="weight_by_zh",
    )(own, *pieces)


def by_xl_body(low, high, beside_low, beside_high, low_ref, high_ref):
    xl = lax.axis_index("xl")
    for mine, beside, out in ((low, beside_low, low_ref), (high, beside_high, high_ref)):
        for place in range(2):
            out[place, xl] = mine[place]
            out[place, 1 - xl] = beside[place]


def by_xl(low, high, beside_low, beside_high):
    shape = (2, 2, *low.shape[1:])
    return pl.pallas_call(
        by_xl_body,
        out_shape=[jax.ShapeDtypeStruct(shape, BF16)] * 2,
        compiler_params=pltpu.CompilerParams(vmem_limit_bytes=VMEM_LIMIT),
        cost_estimate=cost(low.size, low.size * 16),
        name="weight_by_xl",
    )(low, high, beside_low, beside_high)


def stacked(refs):
    return jnp.concatenate([ref[...] for ref in refs], axis=0)


def context_gradient_body(place, *refs):
    images, lows, highs, outs, rows_ref = refs[:4], refs[4:8], refs[8:12], refs[12:16], refs[16]
    seq = images[0].shape[0]

    def gather(weights):
        width = weights[0].shape[1]
        for part, weight in enumerate(weights):
            cols = pl.ds(pl.multiple_of(place[part] * width, 128), width)
            rows_ref[:, cols] = weight[...]

    pl.when(pl.program_id(0) < 2)(functools.partial(gather, lows))
    pl.when(pl.program_id(0) >= 2)(functools.partial(gather, highs))
    total = dot(stacked(images), rows_ref[...], NT)
    for image, out in enumerate(outs):
        out[...] = total[image * seq : (image + 1) * seq].astype(out.dtype)


def context_gradient(places, grads, lows, highs):
    seq, half = grads[0].shape[0], grads[0].shape[1] // 2
    block, width = lows[0].shape[0] // 2, lows[0].shape[1]
    rows = 4 * block
    image = pl.BlockSpec((seq, half), lambda i, place: (0, place[4]))
    low = pl.BlockSpec((block, width), lambda i, place: (jnp.minimum(i, 1), 0))
    high = pl.BlockSpec((block, width), lambda i, place: (jnp.maximum(i - 2, 0), 0))
    out = pl.BlockSpec((seq, block), lambda i, place: (0, i))
    return pl.pallas_call(
        context_gradient_body,
        grid_spec=pltpu.PrefetchScalarGridSpec(
            num_scalar_prefetch=1,
            grid=(4,),
            in_specs=[image] * 4 + [low] * 4 + [high] * 4,
            out_specs=[out] * 4,
            scratch_shapes=[pltpu.VMEM((block, half), BF16)],
        ),
        out_shape=[
            jax.ShapeDtypeStruct((seq, rows), kind) for kind in (F32, BF16, F32, BF16)
        ],
        compiler_params=params(),
        cost_estimate=cost(8 * seq * half * rows, 20 * 2**20),
        name="context_gradient",
    )(places, *grads, *lows, *highs)


def weight_gradient_body(place, c0, c1, c2, c3, d0, d1, d2, d3, out_ref):
    context_t = jnp.concatenate([c[...] for c in (c0, c1, c2, c3)], axis=1)
    part = d0.shape[1] // 2
    for half in range(2):
        cols = slice(half * part, (half + 1) * part)
        grads = jnp.concatenate([d[:, cols] for d in (d0, d1, d2, d3)], axis=0)
        total = dot(context_t, grads, (((1,), (0,)), ((), ())))
        for chip in range(16):
            out_ref[chip, 0, :, cols] = total[chip * 24 : (chip + 1) * 24].astype(BF16)


def weight_gradient(core, contexts, grads):
    rows, seq = contexts[0].shape
    half = grads[0].shape[1] // 2
    return pl.pallas_call(
        weight_gradient_body,
        grid_spec=pltpu.PrefetchScalarGridSpec(
            num_scalar_prefetch=1,
            grid=(4,),
            in_specs=[pl.BlockSpec((rows // 4, seq), lambda i, place: (i, 0))] * 4
            + [pl.BlockSpec((seq, half), lambda i, place: (0, place[0]))] * 4,
            out_specs=pl.BlockSpec((16, 1, 24, half), lambda i, place: (0, i, 0, 0)),
        ),
        out_shape=jax.ShapeDtypeStruct((16, 4, 24, half), BF16),
        compiler_params=params(),
        cost_estimate=cost(8 * seq * half * rows, 12 * 2**20),
        name="weight_gradient",
    )(core, *contexts, *grads)


def sums_on_owners(terms, zh, c):
    sums = jnp.sum(terms.astype(F32), axis=0).astype(BF16)
    mine = lax.dynamic_index_in_dim(sums, zh, 0, False).astype(F32)
    for step in (1, 2, 3):
        away = lax.dynamic_index_in_dim(sums, (zh + step) % 4, 0, False)
        mine = mine + lax.ppermute(away, "zh", ring(4, step)).astype(F32)
    mine = mine.reshape(2, 12, -1)
    kept = jnp.where(c == 0, mine[0], mine[1])
    sent = jnp.where(c == 0, mine[1], mine[0])
    return kept, lax.ppermute(sent, "c", SWAP)


def per_device(queries, keys, values, grad_output, weight_codes, weight_scales):
    _, seq, total = queries.shape
    features = grad_output.shape[2]
    q, k, v = (a.reshape(seq, total) for a in (queries, keys, values))
    grad = grad_output.reshape(seq, features)
    zh, zl, xl, c, y = (lax.axis_index(name) for name in ("zh", "zl", "xl", "c", "y"))
    core = c.astype(jnp.int32).reshape(1)
    width = 384
    own_parity = zl.astype(jnp.int32).reshape(1)
    other_parity = 1 - own_parity

    piece, sent = restore(weight_codes, weight_scales.T)
    arrived = lax.ppermute(sent, "c", SWAP)
    pair = jnp.where(
        c == 0, jnp.concatenate([piece, arrived], 0), jnp.concatenate([arrived, piece], 0)
    )
    behind = [lax.ppermute(pair, "zh", ring(4, step)) for step in (1, 2, 3)]
    (late_parity,) = after((other_parity,), (behind[0],))
    context_other = forward(late_parity, q, k, v, width)
    (pair,) = after((pair,), (context_other,))
    low, high = by_zh(pair, behind)
    beside_low = lax.ppermute(low, ("xl", "xh"), x_ring(1))
    beside_high = lax.ppermute(high, ("xl", "xh"), x_ring(-1))

    d1 = lax.ppermute(grad, "c", SWAP)

    (context_other,) = after((context_other,), (behind[1], behind[2]))
    c2 = lax.ppermute(context_other, "zl", SWAP)

    low, high = by_xl(low, high, beside_low, beside_high)
    low, high = after((low, high), (d1,))
    (sent,) = after((grad,), (c2, low))
    d2 = lax.ppermute(sent, "zl", SWAP)
    (late_parity,) = after((own_parity,), (low,))
    context_own = forward(late_parity, q, k, v, width)
    c1 = lax.ppermute(context_own, "c", SWAP)
    lows, highs = ([piece.reshape(-1, width)] for piece in (low, high))
    for step in (1, -1):
        lows.append(lax.ppermute(lows[0], "y", ring(4, step)))
        highs.append(lax.ppermute(highs[0], "y", ring(4, step)))
    lows.append(lax.ppermute(lows[1], "y", ring(4, 1)))
    highs.append(lax.ppermute(highs[2], "y", ring(4, -1)))
    (sent,) = after((c2,), (lows[1], highs[2]))
    c3 = lax.ppermute(sent, "c", SWAP)
    (sent,) = after((d2,), (c1, c3, lows[2], highs[1]))
    grads = (grad, d1, d2, lax.ppermute(sent, "c", SWAP))

    terms = weight_gradient(core, (context_own, c1, c2, c3), grads)
    (terms,) = after((terms,), (lows[3], highs[3]))
    terms = lax.all_to_all(terms, ("xl", "xh", "y"), 0, 0, tiled=True)

    places = jnp.stack([y, (y + 3) % 4, (y + 1) % 4, (y + 2) % 4, c]).astype(jnp.int32)
    g0, g1, g2, g3 = context_gradient(places, grads, lows, highs)
    r3 = lax.ppermute(g3, "c", SWAP)
    r1 = lax.ppermute(g1, "c", SWAP)
    g_other = lax.ppermute((g2 + r3.astype(F32)).astype(BF16), "zl", SWAP)
    first = backward(own_parity, q, k, v, (g0, r1), width)
    outs = backward(other_parity, q, k, v, (g_other,), width, first)

    (terms,) = after((terms,), tuple(outs))
    kept, got = sums_on_owners(terms, zh, c)
    grad_weight = jnp.where(
        c == 0, jnp.concatenate([kept, got], 1), jnp.concatenate([got, kept], 1)
    )
    return tuple(out.reshape(1, seq, total) for out in outs) + (grad_weight,)


def solution(mesh):
    split = Mesh(mesh.devices.reshape(4, 2, 2, 2, 2, 4), AXES)
    image = P(AXES, None, None)
    return jax.shard_map(
        per_device,
        mesh=split,
        in_specs=(image, image, image, image, P(SHARD, None), P(SHARD, None)),
        out_specs=(image, image, image, P(AXES, None)),
        check_vma=False,
    )
```

```python
import functools

import jax
import jax.numpy as jnp
from jax import lax
from jax.experimental import pallas as pl
from jax.experimental.pallas import tpu as pltpu
from jax.sharding import Mesh
from jax.sharding import PartitionSpec as P

AXES = ("zh", "zl", "xl", "c", "xh", "y")
SHARD = ("zh", "zl", "xl", "c")
HD = 128
SCALE = HD**-0.5
F32 = jnp.float32
BF16 = jnp.bfloat16
SWAP = [(0, 1), (1, 0)]
NT = (((1,), (1,)), ((), ()))
TN = (((0,), (0,)), ((), ()))
VMEM_LIMIT = 60 * 2**20


def ring(count, step):
    return [(i, (i + step) % count) for i in range(count)]


def x_ring(step):
    def place(x):
        return (x % 2) * 2 + x // 2

    return [(place(x), place((x + step) % 4)) for x in range(4)]


def dot(a, b, dims):
    return lax.dot_general(a, b, dims, preferred_element_type=F32)


def params():
    return pltpu.CompilerParams(
        dimension_semantics=("arbitrary",), vmem_limit_bytes=VMEM_LIMIT
    )


def cost(flops, moved, exps=0):
    return pl.CostEstimate(flops=flops, bytes_accessed=moved, transcendentals=exps)


def softmax(q, k):
    scores = dot(q, k, NT) * SCALE
    exponent = jnp.exp(scores - jnp.max(scores, axis=1, keepdims=True))
    return exponent * (1.0 / jnp.sum(exponent, axis=1, keepdims=True))


def forward_body(pick, q_ref, k_ref, v_ref, out_ref, plain, sorted_rows):
    for head in range(q_ref.shape[1] // HD):
        cols = slice(head * HD, (head + 1) * HD)
        probs = softmax(q_ref[:, cols], k_ref[:, cols]).astype(BF16)
        plain[cols, :] = dot(v_ref[:, cols], probs, (((0,), (1,)), ((), ())))
    for xl in range(2):
        for xh in range(2):
            for y in range(4):
                for core in range(2):
                    old = xl * 192 + core * 96 + xh * 48 + y * 12
                    new = xl * 192 + xh * 96 + y * 24 + core * 12
                    sorted_rows[new : new + 12, :] = plain[old : old + 12, :]
    out_ref[...] = sorted_rows[...].astype(BF16)


def forward(parity, q, k, v, width):
    seq, total = q.shape
    blocks = total // width // 2
    spec = pl.BlockSpec((seq, width), lambda i, pick: (0, 2 * i + pick[0]))
    return pl.pallas_call(
        forward_body,
        grid_spec=pltpu.PrefetchScalarGridSpec(
            num_scalar_prefetch=1,
            grid=(blocks,),
            in_specs=[spec] * 3,
            out_specs=pl.BlockSpec((width, seq), lambda i, pick: (i, 0)),
            scratch_shapes=[pltpu.VMEM((width, seq), F32)] * 2,
        ),
        out_shape=jax.ShapeDtypeStruct((total // 2, seq), BF16),
        compiler_params=params(),
        cost_estimate=cost(2 * seq * seq * total, 2 * seq * total * 2, seq * seq * total // HD // 2),
        name="context_half",
    )(parity, q, k, v)


def backward_body(own, pick, q_ref, k_ref, v_ref, *refs):
    if own:
        g_ref, r_ref, gq_ref, gk_ref, gv_ref = refs
    else:
        g_ref, _, _, _, gq_ref, gk_ref, gv_ref = refs
    for head in range(q_ref.shape[1] // HD):
        cols = slice(head * HD, (head + 1) * HD)
        q, k, v = q_ref[:, cols], k_ref[:, cols], v_ref[:, cols]
        if own:
            g = (g_ref[:, cols] + r_ref[:, cols].astype(F32)).astype(BF16)
        else:
            g = g_ref[:, cols]
        probs = softmax(q, k)
        gv_ref[:, cols] = dot(probs.astype(BF16), g, TN).astype(BF16)
        dprobs = dot(g, v, NT)
        delta = jnp.sum(probs * dprobs, axis=1, keepdims=True)
        dscores = (probs * (dprobs - delta) * SCALE).astype(BF16)
        gq_ref[:, cols] = dot(dscores, k, (((1,), (0,)), ((), ()))).astype(BF16)
        gk_ref[:, cols] = dot(dscores, q, TN).astype(BF16)


def backward(parity, q, k, v, grads, width, before=None):
    seq, total = q.shape
    blocks = total // width // 2
    spec = pl.BlockSpec((seq, width), lambda i, pick: (0, 2 * i + pick[0]))
    half = pl.BlockSpec((seq, width), lambda i, pick: (0, i))
    whole = jax.ShapeDtypeStruct((seq, total), BF16)
    extra = [] if before is None else list(before)
    return pl.pallas_call(
        functools.partial(backward_body, before is None),
        grid_spec=pltpu.PrefetchScalarGridSpec(
            num_scalar_prefetch=1,
            grid=(blocks,),
            in_specs=[spec] * 3
            + [half] * len(grads)
            + [pl.BlockSpec(memory_space=pl.ANY)] * len(extra),
            out_specs=[spec] * 3,
        ),
        out_shape=[whole] * 3,
        input_output_aliases={} if before is None else {5: 0, 6: 1, 7: 2},
        compiler_params=params(),
        cost_estimate=cost(5 * seq * seq * total, 7 * seq * total, seq * seq * total // HD // 2),
        name="attention_gradients",
    )(parity, q, k, v, *grads, *extra)


def after(values, events):
    return lax.optimization_barrier((values, events))[0]


def restore_body(codes_ref, scales_ref, near_ref, away_ref):
    core, y = lax.axis_index("c"), lax.axis_index("y")
    blocks = scales_ref.shape[0]
    width = near_ref.shape[1]
    for side, out in ((core, near_ref), (1 - core, away_ref)):
        first = (side * 4 + y) * (width // 128)
        for tile in range(width // 128):
            column = first + tile
            codes = codes_ref[:, pl.ds(pl.multiple_of(column * 128, 128), 128)].astype(F32)
            lane = lax.broadcasted_iota(jnp.int32, (blocks, 128), 0)
            chosen = jnp.where(lane == column // 2, 1.0, 0.0)
            scale = lax.dot_general(
                scales_ref[...],
                chosen,
                TN,
                precision=lax.Precision.HIGHEST,
                preferred_element_type=F32,
            )
            out[:, tile * 128 : (tile + 1) * 128] = (codes * scale).astype(BF16)


def restore(codes, scales):
    rows = codes.shape[0]
    return pl.pallas_call(
        restore_body,
        out_shape=[jax.ShapeDtypeStruct((rows, 384), BF16)] * 2,
        compiler_params=pltpu.CompilerParams(vmem_limit_bytes=8 * 2**20),
        cost_estimate=cost(rows * 768, rows * 3072),
        name="weight_pieces",
    )(codes, scales)


def by_zh_body(own_ref, b1, b2, b3, low_ref, high_ref):
    zh = lax.axis_index("zh")
    for step, piece in enumerate((own_ref, b1, b2, b3)):
        place = lax.rem(zh - step + 4, 4)

        @pl.when(place < 2)
        def _():
            low_ref[place] = piece[...]

        @pl.when(place >= 2)
        def _():
            high_ref[place - 2] = piece[...]


def by_zh(own, pieces):
    return pl.pallas_call(
        by_zh_body,
        in_specs=[pl.BlockSpec(memory_space=pltpu.VMEM)] * 4,
        out_specs=[pl.BlockSpec(memory_space=pltpu.VMEM)] * 2,
        out_shape=[jax.ShapeDtypeStruct((2, *own.shape), BF16)] * 2,
        compiler_params=pltpu.CompilerParams(vmem_limit_bytes=8 * 2**20),
        cost_estimate=cost(own.size, own.size * 16),
        name="weight_by_zh",
    )(own, *pieces)


def by_xl_body(low, high, beside_low, beside_high, low_ref, high_ref):
    xl = lax.axis_index("xl")
    for mine, beside, out in ((low, beside_low, low_ref), (high, beside_high, high_ref)):
        for place in range(2):
            out[place, xl] = mine[place]
            out[place, 1 - xl] = beside[place]


def by_xl(low, high, beside_low, beside_high):
    shape = (2, 2, *low.shape[1:])
    return pl.pallas_call(
        by_xl_body,
        in_specs=[pl.BlockSpec(memory_space=pltpu.VMEM)] * 4,
        out_specs=[pl.BlockSpec(memory_space=pltpu.VMEM)] * 2,
        out_shape=[jax.ShapeDtypeStruct(shape, BF16)] * 2,
        compiler_params=pltpu.CompilerParams(vmem_limit_bytes=8 * 2**20),
        cost_estimate=cost(low.size, low.size * 16),
        name="weight_by_xl",
    )(low, high, beside_low, beside_high)


def stacked(refs):
    return jnp.concatenate([ref[...] for ref in refs], axis=0)


def context_gradient_body(place, *refs):
    images, lows, highs, outs, rows_ref = refs[:4], refs[4:8], refs[8:12], refs[12:16], refs[16]
    seq = images[0].shape[0]

    def gather(weights):
        width = weights[0].shape[1]
        for part, weight in enumerate(weights):
            cols = pl.ds(pl.multiple_of(place[part] * width, 128), width)
            rows_ref[:, cols] = weight[...]

    pl.when(pl.program_id(0) < 2)(functools.partial(gather, lows))
    pl.when(pl.program_id(0) >= 2)(functools.partial(gather, highs))
    total = dot(stacked(images), rows_ref[...], NT)
    for image, out in enumerate(outs):
        out[...] = total[image * seq : (image + 1) * seq].astype(out.dtype)


def context_gradient(places, grads, lows, highs):
    seq, half = grads[0].shape
    block, width = lows[0].shape[0] // 2, lows[0].shape[1]
    rows = 4 * block
    image = pl.BlockSpec((seq, half), lambda i, place: (0, 0))
    low = pl.BlockSpec((block, width), lambda i, place: (jnp.minimum(i, 1), 0))
    high = pl.BlockSpec((block, width), lambda i, place: (jnp.maximum(i - 2, 0), 0))
    out = pl.BlockSpec((seq, block), lambda i, place: (0, i))
    return pl.pallas_call(
        context_gradient_body,
        grid_spec=pltpu.PrefetchScalarGridSpec(
            num_scalar_prefetch=1,
            grid=(4,),
            in_specs=[image] * 4 + [low] * 4 + [high] * 4,
            out_specs=[out] * 4,
            scratch_shapes=[pltpu.VMEM((block, half), BF16)],
        ),
        out_shape=[
            jax.ShapeDtypeStruct((seq, rows), kind) for kind in (F32, BF16, F32, BF16)
        ],
        compiler_params=params(),
        cost_estimate=cost(8 * seq * half * rows, 20 * 2**20),
        name="context_gradient",
    )(places, *grads, *lows, *highs)


def weight_gradient_body(c0, c1, c2, c3, d0, d1, d2, d3, out_ref):
    context_t = jnp.concatenate([c[...] for c in (c0, c1, c2, c3)], axis=1)
    part = d0.shape[1] // 2
    for half in range(2):
        cols = slice(half * part, (half + 1) * part)
        grads = jnp.concatenate([d[:, cols] for d in (d0, d1, d2, d3)], axis=0)
        total = dot(context_t, grads, (((1,), (0,)), ((), ())))
        for chip in range(16):
            out_ref[chip, 0, :, cols] = total[chip * 24 : (chip + 1) * 24].astype(BF16)


def weight_gradient(contexts, grads):
    rows, seq = contexts[0].shape
    half = grads[0].shape[1]
    return pl.pallas_call(
        weight_gradient_body,
        grid=(4,),
        in_specs=[pl.BlockSpec((rows // 4, seq), lambda i: (i, 0))] * 4
        + [pl.BlockSpec((seq, half), lambda i: (0, 0))] * 4,
        out_specs=pl.BlockSpec((16, 1, 24, half), lambda i: (0, i, 0, 0)),
        out_shape=jax.ShapeDtypeStruct((16, 4, 24, half), BF16),
        compiler_params=params(),
        cost_estimate=cost(8 * seq * half * rows, 12 * 2**20),
        name="weight_gradient",
    )(*contexts, *grads)


def sums_on_owners(terms, zh, c):
    sums = jnp.sum(terms.astype(F32), axis=0).astype(BF16)
    mine = lax.dynamic_index_in_dim(sums, zh, 0, False).astype(F32)
    for step in (1, 2, 3):
        away = lax.dynamic_index_in_dim(sums, (zh + step) % 4, 0, False)
        mine = mine + lax.ppermute(away, "zh", ring(4, step)).astype(F32)
    mine = mine.reshape(2, 12, -1)
    kept = jnp.where(c == 0, mine[0], mine[1])
    sent = jnp.where(c == 0, mine[1], mine[0])
    return kept, lax.ppermute(sent, "c", SWAP)


def per_device(queries, keys, values, grad_output, weight_codes, weight_scales):
    _, seq, total = queries.shape
    features = grad_output.shape[2]
    q, k, v = (a.reshape(seq, total) for a in (queries, keys, values))
    grad = grad_output.reshape(seq, features)
    zh, zl, xl, c, y = (lax.axis_index(name) for name in ("zh", "zl", "xl", "c", "y"))
    width = 384
    own_parity = zl.astype(jnp.int32).reshape(1)
    other_parity = 1 - own_parity

    piece, sent = restore(weight_codes, weight_scales.T)
    arrived = lax.ppermute(sent, "c", SWAP)
    pair = jnp.where(
        c == 0, jnp.concatenate([piece, arrived], 0), jnp.concatenate([arrived, piece], 0)
    )
    behind = [lax.ppermute(pair, "zh", ring(4, step)) for step in (1, 2, 3)]
    (late_parity,) = after((other_parity,), (behind[0],))
    context_other = forward(late_parity, q, k, v, width)
    (pair,) = after((pair,), (context_other,))
    low, high = by_zh(pair, behind)
    beside_low = lax.ppermute(low, ("xl", "xh"), x_ring(1))
    beside_high = lax.ppermute(high, ("xl", "xh"), x_ring(-1))

    half = features // 2
    (late_grad,) = after((grad,), (context_other,))
    mine, other = (
        lax.dynamic_slice_in_dim(late_grad, side * half, half, 1) for side in (c, 1 - c)
    )
    d1 = lax.ppermute(other, "c", SWAP)

    (context_other,) = after((context_other,), (behind[1], behind[2]))
    c2 = lax.ppermute(context_other, "zl", SWAP)

    low, high = by_xl(low, high, beside_low, beside_high)
    near, diagonal = after((mine, other), (c2, low, d1))
    d2 = lax.ppermute(near, "zl", SWAP)
    d3 = lax.ppermute(diagonal, ("zl", "c"), [(i, 3 - i) for i in range(4)])
    grads = (mine, d1, d2, d3)
    (late_parity,) = after((own_parity,), (low,))
    context_own = forward(late_parity, q, k, v, width)
    lows, highs = ([piece.reshape(-1, width)] for piece in (low, high))
    for step in (1, -1):
        lows.append(lax.ppermute(lows[0], "y", ring(4, step)))
        highs.append(lax.ppermute(highs[0], "y", ring(4, step)))
    lows.append(lax.ppermute(lows[1], "y", ring(4, 1)))
    highs.append(lax.ppermute(highs[2], "y", ring(4, -1)))
    sent_own, sent_away = after((context_own, c2), (*lows[1:3], *highs[1:3]))
    c1 = lax.ppermute(sent_own, "c", SWAP)
    c3 = lax.ppermute(sent_away, "c", SWAP)

    terms = weight_gradient((context_own, c1, c2, c3), grads)
    (terms,) = after((terms,), (*lows[2:], *highs[1:]))
    terms = lax.all_to_all(terms, ("xl", "xh", "y"), 0, 0, tiled=True)

    places = jnp.stack([y, (y + 3) % 4, (y + 1) % 4, (y + 2) % 4]).astype(jnp.int32)
    g0, g1, g2, g3 = context_gradient(places, grads, lows, highs)
    r3 = lax.ppermute(g3, "c", SWAP)
    r1 = lax.ppermute(g1, "c", SWAP)
    g_other = lax.ppermute((g2 + r3.astype(F32)).astype(BF16), "zl", SWAP)
    first = backward(own_parity, q, k, v, (g0, r1), width)
    outs = backward(other_parity, q, k, v, (g_other,), width, first)

    (terms,) = after((terms,), tuple(outs))
    kept, got = sums_on_owners(terms, zh, c)
    grad_weight = jnp.where(
        c == 0, jnp.concatenate([kept, got], 1), jnp.concatenate([got, kept], 1)
    )
    return tuple(out.reshape(1, seq, total) for out in outs) + (grad_weight,)


def solution(mesh):
    split = Mesh(mesh.devices.reshape(4, 2, 2, 2, 2, 4), AXES)
    image = P(AXES, None, None)
    return jax.shard_map(
        per_device,
        mesh=split,
        in_specs=(image, image, image, image, P(SHARD, None), P(SHARD, None)),
        out_specs=(image, image, image, P(AXES, None)),
        check_vma=False,
    )
```

```python
import functools

import jax
import jax.numpy as jnp
from jax import lax
from jax.experimental import pallas as pl
from jax.experimental.pallas import tpu as pltpu
from jax.sharding import Mesh
from jax.sharding import PartitionSpec as P

AXES = ("zh", "zl", "xl", "c", "xh", "y")
SHARD = ("zh", "zl", "xl", "c")
HD = 128
SCALE = HD**-0.5
F32 = jnp.float32
BF16 = jnp.bfloat16
SWAP = [(0, 1), (1, 0)]
NT = (((1,), (1,)), ((), ()))
TN = (((0,), (0,)), ((), ()))
VMEM_LIMIT = 60 * 2**20


def ring(count, step):
    return [(i, (i + step) % count) for i in range(count)]


def x_ring(step):
    def place(x):
        return (x % 2) * 2 + x // 2

    return [(place(x), place((x + step) % 4)) for x in range(4)]


def dot(a, b, dims):
    return lax.dot_general(a, b, dims, preferred_element_type=F32)


def params():
    return pltpu.CompilerParams(
        dimension_semantics=("arbitrary",), vmem_limit_bytes=VMEM_LIMIT
    )


def cost(flops, moved, exps=0):
    return pl.CostEstimate(flops=flops, bytes_accessed=moved, transcendentals=exps)


def softmax(q, k):
    scores = dot(q, k, NT) * SCALE
    exponent = jnp.exp(scores - jnp.max(scores, axis=1, keepdims=True))
    return exponent * (1.0 / jnp.sum(exponent, axis=1, keepdims=True))


def forward_body(pick, q_ref, k_ref, v_ref, out_ref, plain, sorted_rows):
    for head in range(q_ref.shape[1] // HD):
        cols = slice(head * HD, (head + 1) * HD)
        probs = softmax(q_ref[:, cols], k_ref[:, cols]).astype(BF16)
        plain[cols, :] = dot(v_ref[:, cols], probs, (((0,), (1,)), ((), ())))
    for xl in range(2):
        for xh in range(2):
            for y in range(4):
                for core in range(2):
                    old = xl * 192 + core * 96 + xh * 48 + y * 12
                    new = xl * 192 + xh * 96 + y * 24 + core * 12
                    sorted_rows[new : new + 12, :] = plain[old : old + 12, :]
    out_ref[...] = sorted_rows[...].astype(BF16)


def forward(parity, q, k, v, width):
    seq, total = q.shape
    blocks = total // width // 2
    spec = pl.BlockSpec((seq, width), lambda i, pick: (0, 2 * i + pick[0]))
    return pl.pallas_call(
        forward_body,
        grid_spec=pltpu.PrefetchScalarGridSpec(
            num_scalar_prefetch=1,
            grid=(blocks,),
            in_specs=[spec] * 3,
            out_specs=pl.BlockSpec((width, seq), lambda i, pick: (i, 0)),
            scratch_shapes=[pltpu.VMEM((width, seq), F32)] * 2,
        ),
        out_shape=jax.ShapeDtypeStruct((total // 2, seq), BF16),
        compiler_params=params(),
        cost_estimate=cost(2 * seq * seq * total, 2 * seq * total * 2, seq * seq * total // HD // 2),
        name="context_half",
    )(parity, q, k, v)


def backward_body(own, pick, q_ref, k_ref, v_ref, *refs):
    if own:
        g_ref, r_ref, gq_ref, gk_ref, gv_ref = refs
    else:
        g_ref, _, _, _, gq_ref, gk_ref, gv_ref = refs
    for head in range(q_ref.shape[1] // HD):
        cols = slice(head * HD, (head + 1) * HD)
        q, k, v = q_ref[:, cols], k_ref[:, cols], v_ref[:, cols]
        if own:
            g = (g_ref[:, cols] + r_ref[:, cols].astype(F32)).astype(BF16)
        else:
            g = g_ref[:, cols]
        probs = softmax(q, k)
        gv_ref[:, cols] = dot(probs.astype(BF16), g, TN).astype(BF16)
        dprobs = dot(g, v, NT)
        delta = jnp.sum(probs * dprobs, axis=1, keepdims=True)
        dscores = (probs * (dprobs - delta) * SCALE).astype(BF16)
        gq_ref[:, cols] = dot(dscores, k, (((1,), (0,)), ((), ()))).astype(BF16)
        gk_ref[:, cols] = dot(dscores, q, TN).astype(BF16)


def backward(parity, q, k, v, grads, width, before=None):
    seq, total = q.shape
    blocks = total // width // 2
    spec = pl.BlockSpec((seq, width), lambda i, pick: (0, 2 * i + pick[0]))
    half = pl.BlockSpec((seq, width), lambda i, pick: (0, i))
    whole = jax.ShapeDtypeStruct((seq, total), BF16)
    extra = [] if before is None else list(before)
    return pl.pallas_call(
        functools.partial(backward_body, before is None),
        grid_spec=pltpu.PrefetchScalarGridSpec(
            num_scalar_prefetch=1,
            grid=(blocks,),
            in_specs=[spec] * 3
            + [half] * len(grads)
            + [pl.BlockSpec(memory_space=pl.ANY)] * len(extra),
            out_specs=[spec] * 3,
        ),
        out_shape=[whole] * 3,
        input_output_aliases={} if before is None else {5: 0, 6: 1, 7: 2},
        compiler_params=params(),
        cost_estimate=cost(5 * seq * seq * total, 7 * seq * total, seq * seq * total // HD // 2),
        name="attention_gradients",
    )(parity, q, k, v, *grads, *extra)


def after(values, events):
    return lax.optimization_barrier((values, events))[0]


def restore_body(codes_ref, scales_ref, near_ref, away_ref):
    core, y = lax.axis_index("c"), lax.axis_index("y")
    blocks = scales_ref.shape[0]
    width = near_ref.shape[1]
    for side, out in ((core, near_ref), (1 - core, away_ref)):
        first = (side * 4 + y) * (width // 128)
        for tile in range(width // 128):
            column = first + tile
            codes = codes_ref[:, pl.ds(pl.multiple_of(column * 128, 128), 128)].astype(F32)
            lane = lax.broadcasted_iota(jnp.int32, (blocks, 128), 0)
            chosen = jnp.where(lane == column // 2, 1.0, 0.0)
            scale = lax.dot_general(
                scales_ref[...],
                chosen,
                TN,
                precision=lax.Precision.HIGHEST,
                preferred_element_type=F32,
            )
            out[:, tile * 128 : (tile + 1) * 128] = (codes * scale).astype(BF16)


def restore(codes, scales):
    rows = codes.shape[0]
    return pl.pallas_call(
        restore_body,
        out_shape=[jax.ShapeDtypeStruct((rows, 384), BF16)] * 2,
        compiler_params=pltpu.CompilerParams(vmem_limit_bytes=8 * 2**20),
        cost_estimate=cost(rows * 768, rows * 3072),
        name="weight_pieces",
    )(codes, scales)


def by_zh_body(own_ref, b1, b2, b3, low_ref, high_ref):
    zh = lax.axis_index("zh")
    for step, piece in enumerate((own_ref, b1, b2, b3)):
        place = lax.rem(zh - step + 4, 4)

        @pl.when(place < 2)
        def _():
            low_ref[place] = piece[...]

        @pl.when(place >= 2)
        def _():
            high_ref[place - 2] = piece[...]


def by_zh(own, pieces):
    return pl.pallas_call(
        by_zh_body,
        in_specs=[pl.BlockSpec(memory_space=pltpu.VMEM)] * 4,
        out_specs=[pl.BlockSpec(memory_space=pltpu.VMEM)] * 2,
        out_shape=[jax.ShapeDtypeStruct((2, *own.shape), BF16)] * 2,
        compiler_params=pltpu.CompilerParams(vmem_limit_bytes=8 * 2**20),
        cost_estimate=cost(own.size, own.size * 16),
        name="weight_by_zh",
    )(own, *pieces)


def by_xl_body(low, high, beside_low, beside_high, low_ref, high_ref):
    xl = lax.axis_index("xl")
    for mine, beside, out in ((low, beside_low, low_ref), (high, beside_high, high_ref)):
        for place in range(2):
            out[place, xl] = mine[place]
            out[place, 1 - xl] = beside[place]


def by_xl(low, high, beside_low, beside_high):
    shape = (2, 2, *low.shape[1:])
    return pl.pallas_call(
        by_xl_body,
        in_specs=[pl.BlockSpec(memory_space=pltpu.VMEM)] * 4,
        out_specs=[pl.BlockSpec(memory_space=pltpu.VMEM)] * 2,
        out_shape=[jax.ShapeDtypeStruct(shape, BF16)] * 2,
        compiler_params=pltpu.CompilerParams(vmem_limit_bytes=8 * 2**20),
        cost_estimate=cost(low.size, low.size * 16),
        name="weight_by_xl",
    )(low, high, beside_low, beside_high)


def stacked(refs):
    return jnp.concatenate([ref[...] for ref in refs], axis=0)


def context_gradient_body(place, *refs):
    images, lows, highs, outs, rows_ref = refs[:4], refs[4:8], refs[8:12], refs[12:16], refs[16]
    seq = images[0].shape[0]

    def gather(weights):
        width = weights[0].shape[1]
        for part, weight in enumerate(weights):
            cols = pl.ds(pl.multiple_of(place[part] * width, 128), width)
            rows_ref[:, cols] = weight[...]

    pl.when(pl.program_id(0) < 2)(functools.partial(gather, lows))
    pl.when(pl.program_id(0) >= 2)(functools.partial(gather, highs))
    total = dot(stacked(images), rows_ref[...], NT)
    for image, out in enumerate(outs):
        out[...] = total[image * seq : (image + 1) * seq].astype(out.dtype)


def context_gradient(places, grads, lows, highs):
    seq, half = grads[0].shape
    block, width = lows[0].shape[0] // 2, lows[0].shape[1]
    rows = 4 * block
    image = pl.BlockSpec((seq, half), lambda i, place: (0, 0))
    low = pl.BlockSpec((block, width), lambda i, place: (jnp.minimum(i, 1), 0))
    high = pl.BlockSpec((block, width), lambda i, place: (jnp.maximum(i - 2, 0), 0))
    out = pl.BlockSpec((seq, block), lambda i, place: (0, i))
    return pl.pallas_call(
        context_gradient_body,
        grid_spec=pltpu.PrefetchScalarGridSpec(
            num_scalar_prefetch=1,
            grid=(4,),
            in_specs=[image] * 4 + [low] * 4 + [high] * 4,
            out_specs=[out] * 4,
            scratch_shapes=[pltpu.VMEM((block, half), BF16)],
        ),
        out_shape=[
            jax.ShapeDtypeStruct((seq, rows), kind) for kind in (F32, BF16, F32, BF16)
        ],
        compiler_params=params(),
        cost_estimate=cost(8 * seq * half * rows, 20 * 2**20),
        name="context_gradient",
    )(places, *grads, *lows, *highs)


def weight_gradient_body(c0, c1, c2, c3, d0, d1, d2, d3, out_ref):
    context_t = jnp.concatenate([c[...] for c in (c0, c1, c2, c3)], axis=1)
    total = dot(context_t, stacked((d0, d1, d2, d3)), (((1,), (0,)), ((), ())))
    block = context_t.shape[0] // 4
    for place in range(4):
        for chip in range(16):
            first = place * block + chip * 24
            out_ref[chip, place] = total[first : first + 24].astype(BF16)


def weight_gradient(contexts, grads):
    rows, seq = contexts[0].shape
    half = grads[0].shape[1]
    width = half // 4
    return pl.pallas_call(
        weight_gradient_body,
        grid=(4,),
        in_specs=[pl.BlockSpec((rows, seq), lambda i: (0, 0))] * 4
        + [pl.BlockSpec((seq, width), lambda i: (0, i))] * 4,
        out_specs=pl.BlockSpec((16, 4, 24, width), lambda i: (0, 0, 0, i)),
        out_shape=jax.ShapeDtypeStruct((16, 4, 24, half), BF16),
        compiler_params=params(),
        cost_estimate=cost(8 * seq * half * rows, 12 * 2**20),
        name="weight_gradient",
    )(*contexts, *grads)


def sums_on_owners(terms, zh, c):
    sums = jnp.sum(terms.astype(F32), axis=0).astype(BF16)
    mine = lax.dynamic_index_in_dim(sums, zh, 0, False).astype(F32)
    for step in (1, 2, 3):
        away = lax.dynamic_index_in_dim(sums, (zh + step) % 4, 0, False)
        mine = mine + lax.ppermute(away, "zh", ring(4, step)).astype(F32)
    mine = mine.reshape(2, 12, -1)
    kept = jnp.where(c == 0, mine[0], mine[1])
    sent = jnp.where(c == 0, mine[1], mine[0])
    return kept, lax.ppermute(sent, "c", SWAP)


def per_device(queries, keys, values, grad_output, weight_codes, weight_scales):
    _, seq, total = queries.shape
    features = grad_output.shape[2]
    q, k, v = (a.reshape(seq, total) for a in (queries, keys, values))
    grad = grad_output.reshape(seq, features)
    zh, zl, xl, c, y = (lax.axis_index(name) for name in ("zh", "zl", "xl", "c", "y"))
    width = 384
    own_parity = zl.astype(jnp.int32).reshape(1)
    other_parity = 1 - own_parity

    piece, sent = restore(weight_codes, weight_scales.T)
    arrived = lax.ppermute(sent, "c", SWAP)
    pair = jnp.where(
        c == 0, jnp.concatenate([piece, arrived], 0), jnp.concatenate([arrived, piece], 0)
    )
    behind = [lax.ppermute(pair, "zh", ring(4, step)) for step in (1, 2, 3)]
    (late_parity,) = after((other_parity,), (behind[0],))
    context_other = forward(late_parity, q, k, v, width)
    (pair,) = after((pair,), (context_other,))
    low, high = by_zh(pair, behind)
    beside_low = lax.ppermute(low, ("xl", "xh"), x_ring(1))
    beside_high = lax.ppermute(high, ("xl", "xh"), x_ring(-1))

    half = features // 2
    (late_grad,) = after((grad,), (context_other,))
    mine, other = (
        lax.dynamic_slice_in_dim(late_grad, side * half, half, 1) for side in (c, 1 - c)
    )
    d1 = lax.ppermute(other, "c", SWAP)

    (context_other,) = after((context_other,), (behind[1], behind[2]))
    c2 = lax.ppermute(context_other, "zl", SWAP)

    low, high = by_xl(low, high, beside_low, beside_high)
    near, diagonal = after((mine, other), (c2, low, d1))
    d2 = lax.ppermute(near, "zl", SWAP)
    d3 = lax.ppermute(diagonal, ("zl", "c"), [(i, 3 - i) for i in range(4)])
    grads = (mine, d1, d2, d3)
    (late_parity,) = after((own_parity,), (low,))
    context_own = forward(late_parity, q, k, v, width)
    lows, highs = ([piece.reshape(-1, width)] for piece in (low, high))
    for step in (1, -1):
        lows.append(lax.ppermute(lows[0], "y", ring(4, step)))
        highs.append(lax.ppermute(highs[0], "y", ring(4, step)))
    lows.append(lax.ppermute(lows[1], "y", ring(4, 1)))
    highs.append(lax.ppermute(highs[2], "y", ring(4, -1)))
    sent_own, sent_away = after((context_own, c2), (*lows[1:3], *highs[1:3]))
    c1 = lax.ppermute(sent_own, "c", SWAP)
    c3 = lax.ppermute(sent_away, "c", SWAP)

    terms = weight_gradient((context_own, c1, c2, c3), grads)
    (terms,) = after((terms,), (*lows[2:], *highs[1:]))
    terms = lax.all_to_all(terms, ("xl", "xh", "y"), 0, 0, tiled=True)

    places = jnp.stack([y, (y + 3) % 4, (y + 1) % 4, (y + 2) % 4]).astype(jnp.int32)
    g0, g1, g2, g3 = context_gradient(places, grads, lows, highs)
    r3 = lax.ppermute(g3, "c", SWAP)
    r1 = lax.ppermute(g1, "c", SWAP)
    g_other = lax.ppermute((g2 + r3.astype(F32)).astype(BF16), "zl", SWAP)
    first = backward(own_parity, q, k, v, (g0, r1), width)
    outs = backward(other_parity, q, k, v, (g_other,), width, first)

    (terms,) = after((terms,), tuple(outs))
    kept, got = sums_on_owners(terms, zh, c)
    grad_weight = jnp.where(
        c == 0, jnp.concatenate([kept, got], 1), jnp.concatenate([got, kept], 1)
    )
    return tuple(out.reshape(1, seq, total) for out in outs) + (grad_weight,)


def solution(mesh):
    split = Mesh(mesh.devices.reshape(4, 2, 2, 2, 2, 4), AXES)
    image = P(AXES, None, None)
    return jax.shard_map(
        per_device,
        mesh=split,
        in_specs=(image, image, image, image, P(SHARD, None), P(SHARD, None)),
        out_specs=(image, image, image, P(AXES, None)),
        check_vma=False,
    )
```

```python
import functools

import jax
import jax.numpy as jnp
from jax import lax
from jax.experimental import pallas as pl
from jax.experimental.pallas import tpu as pltpu
from jax.sharding import Mesh
from jax.sharding import PartitionSpec as P

AXES = ("zh", "zl", "xl", "c", "xh", "y")
SHARD = ("zh", "zl", "xl", "c")
HD = 128
SCALE = HD**-0.5
F32 = jnp.float32
BF16 = jnp.bfloat16
SWAP = [(0, 1), (1, 0)]
NT = (((1,), (1,)), ((), ()))
TN = (((0,), (0,)), ((), ()))
VMEM_LIMIT = 60 * 2**20


def ring(count, step):
    return [(i, (i + step) % count) for i in range(count)]


def x_ring(step):
    def place(x):
        return (x % 2) * 2 + x // 2

    return [(place(x), place((x + step) % 4)) for x in range(4)]


def dot(a, b, dims):
    return lax.dot_general(a, b, dims, preferred_element_type=F32)


def params():
    return pltpu.CompilerParams(
        dimension_semantics=("arbitrary",), vmem_limit_bytes=VMEM_LIMIT
    )


def cost(flops, moved, exps=0):
    return pl.CostEstimate(flops=flops, bytes_accessed=moved, transcendentals=exps)


def softmax(q, k):
    scores = dot(q, k, NT) * SCALE
    exponent = jnp.exp(scores - jnp.max(scores, axis=1, keepdims=True))
    return exponent * (1.0 / jnp.sum(exponent, axis=1, keepdims=True))


def forward_body(pick, q_ref, k_ref, v_ref, out_ref, plain, sorted_rows):
    for head in range(q_ref.shape[1] // HD):
        cols = slice(head * HD, (head + 1) * HD)
        probs = softmax(q_ref[:, cols], k_ref[:, cols]).astype(BF16)
        plain[cols, :] = dot(v_ref[:, cols], probs, (((0,), (1,)), ((), ())))
    for xl in range(2):
        for xh in range(2):
            for y in range(4):
                for core in range(2):
                    old = xl * 192 + core * 96 + xh * 48 + y * 12
                    new = xl * 192 + xh * 96 + y * 24 + core * 12
                    sorted_rows[new : new + 12, :] = plain[old : old + 12, :]
    out_ref[...] = sorted_rows[...].astype(BF16)


def forward(parity, q, k, v, width):
    seq, total = q.shape
    blocks = total // width // 2
    spec = pl.BlockSpec((seq, width), lambda i, pick: (0, 2 * i + pick[0]))
    return pl.pallas_call(
        forward_body,
        grid_spec=pltpu.PrefetchScalarGridSpec(
            num_scalar_prefetch=1,
            grid=(blocks,),
            in_specs=[spec] * 3,
            out_specs=pl.BlockSpec((width, seq), lambda i, pick: (i, 0)),
            scratch_shapes=[pltpu.VMEM((width, seq), F32)] * 2,
        ),
        out_shape=jax.ShapeDtypeStruct((total // 2, seq), BF16),
        compiler_params=params(),
        cost_estimate=cost(2 * seq * seq * total, 2 * seq * total * 2, seq * seq * total // HD // 2),
        name="context_half",
    )(parity, q, k, v)


def backward_body(own, pick, q_ref, k_ref, v_ref, *refs):
    if own:
        g_ref, r_ref, gq_ref, gk_ref, gv_ref = refs
    else:
        g_ref, _, _, _, gq_ref, gk_ref, gv_ref = refs
    for head in range(q_ref.shape[1] // HD):
        cols = slice(head * HD, (head + 1) * HD)
        q, k, v = q_ref[:, cols], k_ref[:, cols], v_ref[:, cols]
        if own:
            g = (g_ref[:, cols] + r_ref[:, cols].astype(F32)).astype(BF16)
        else:
            g = g_ref[:, cols]
        probs = softmax(q, k)
        gv_ref[:, cols] = dot(probs.astype(BF16), g, TN).astype(BF16)
        dprobs = dot(g, v, NT)
        delta = jnp.sum(probs * dprobs, axis=1, keepdims=True)
        dscores = (probs * (dprobs - delta) * SCALE).astype(BF16)
        gq_ref[:, cols] = dot(dscores, k, (((1,), (0,)), ((), ()))).astype(BF16)
        gk_ref[:, cols] = dot(dscores, q, TN).astype(BF16)


def backward(parity, q, k, v, grads, width, before=None):
    seq, total = q.shape
    blocks = total // width // 2
    spec = pl.BlockSpec((seq, width), lambda i, pick: (0, 2 * i + pick[0]))
    half = pl.BlockSpec((seq, width), lambda i, pick: (0, i))
    whole = jax.ShapeDtypeStruct((seq, total), BF16)
    extra = [] if before is None else list(before)
    return pl.pallas_call(
        functools.partial(backward_body, before is None),
        grid_spec=pltpu.PrefetchScalarGridSpec(
            num_scalar_prefetch=1,
            grid=(blocks,),
            in_specs=[spec] * 3
            + [half] * len(grads)
            + [pl.BlockSpec(memory_space=pl.ANY)] * len(extra),
            out_specs=[spec] * 3,
        ),
        out_shape=[whole] * 3,
        input_output_aliases={} if before is None else {5: 0, 6: 1, 7: 2},
        compiler_params=params(),
        cost_estimate=cost(5 * seq * seq * total, 7 * seq * total, seq * seq * total // HD // 2),
        name="attention_gradients",
    )(parity, q, k, v, *grads, *extra)


def after(values, events):
    return lax.optimization_barrier((values, events))[0]


def restore_body(codes_ref, scales_ref, near_ref, away_ref):
    core, y = lax.axis_index("c"), lax.axis_index("y")
    blocks = scales_ref.shape[0]
    width = near_ref.shape[1]
    for side, out in ((core, near_ref), (1 - core, away_ref)):
        first = (side * 4 + y) * (width // 128)
        for tile in range(width // 128):
            column = first + tile
            codes = codes_ref[:, pl.ds(pl.multiple_of(column * 128, 128), 128)].astype(F32)
            lane = lax.broadcasted_iota(jnp.int32, (blocks, 128), 0)
            chosen = jnp.where(lane == column // 2, 1.0, 0.0)
            scale = lax.dot_general(
                scales_ref[...],
                chosen,
                TN,
                precision=lax.Precision.HIGHEST,
                preferred_element_type=F32,
            )
            out[:, tile * 128 : (tile + 1) * 128] = (codes * scale).astype(BF16)


def restore(codes, scales):
    rows = codes.shape[0]
    return pl.pallas_call(
        restore_body,
        out_shape=[jax.ShapeDtypeStruct((rows, 384), BF16)] * 2,
        compiler_params=pltpu.CompilerParams(vmem_limit_bytes=8 * 2**20),
        cost_estimate=cost(rows * 768, rows * 3072),
        name="weight_pieces",
    )(codes, scales)


def by_zh_body(own_ref, lower_ref, upper_ref, far_a, far_b, low_ref, high_ref):
    zh = lax.axis_index("zh")
    half = far_a.shape[0]
    for step, piece in ((0, own_ref), (3, lower_ref), (1, upper_ref), (2, None)):
        place = lax.rem(zh + step, 4)

        def put(out, index):
            if piece is None:
                out[index, :half] = far_a[...]
                out[index, half:] = far_b[...]
            else:
                out[index] = piece[...]

        pl.when(place < 2)(lambda: put(low_ref, place))
        pl.when(place >= 2)(lambda: put(high_ref, place - 2))


def by_zh(own, pieces):
    return pl.pallas_call(
        by_zh_body,
        in_specs=[pl.BlockSpec(memory_space=pltpu.VMEM)] * 5,
        out_specs=[pl.BlockSpec(memory_space=pltpu.VMEM)] * 2,
        out_shape=[jax.ShapeDtypeStruct((2, *own.shape), BF16)] * 2,
        compiler_params=pltpu.CompilerParams(vmem_limit_bytes=8 * 2**20),
        cost_estimate=cost(own.size, own.size * 16),
        name="weight_by_zh",
    )(own, *pieces)


def by_xl_body(low, high, beside_low, beside_high, low_ref, high_ref):
    xl = lax.axis_index("xl")
    for mine, beside, out in ((low, beside_low, low_ref), (high, beside_high, high_ref)):
        for place in range(2):
            out[place, xl] = mine[place]
            out[place, 1 - xl] = beside[place]


def by_xl(low, high, beside_low, beside_high):
    shape = (2, 2, *low.shape[1:])
    return pl.pallas_call(
        by_xl_body,
        in_specs=[pl.BlockSpec(memory_space=pltpu.VMEM)] * 4,
        out_specs=[pl.BlockSpec(memory_space=pltpu.VMEM)] * 2,
        out_shape=[jax.ShapeDtypeStruct(shape, BF16)] * 2,
        compiler_params=pltpu.CompilerParams(vmem_limit_bytes=8 * 2**20),
        cost_estimate=cost(low.size, low.size * 16),
        name="weight_by_xl",
    )(low, high, beside_low, beside_high)


def stacked(refs):
    return jnp.concatenate([ref[...] for ref in refs], axis=0)


def context_gradient_body(place, *refs):
    images, lows, highs, outs, rows_ref = refs[:4], refs[4:8], refs[8:12], refs[12:16], refs[16]
    seq = images[0].shape[0]

    def gather(weights):
        width = weights[0].shape[1]
        for part, weight in enumerate(weights):
            cols = pl.ds(pl.multiple_of(place[part] * width, 128), width)
            rows_ref[:, cols] = weight[...]

    pl.when(pl.program_id(0) < 2)(functools.partial(gather, lows))
    pl.when(pl.program_id(0) >= 2)(functools.partial(gather, highs))
    total = dot(stacked(images), rows_ref[...], NT)
    for image, out in enumerate(outs):
        out[...] = total[image * seq : (image + 1) * seq].astype(out.dtype)


def context_gradient(places, grads, lows, highs):
    seq, half = grads[0].shape
    block, width = lows[0].shape[0] // 2, lows[0].shape[1]
    rows = 4 * block
    image = pl.BlockSpec((seq, half), lambda i, place: (0, 0))
    low = pl.BlockSpec((block, width), lambda i, place: (jnp.minimum(i, 1), 0))
    high = pl.BlockSpec((block, width), lambda i, place: (jnp.maximum(i - 2, 0), 0))
    out = pl.BlockSpec((seq, block), lambda i, place: (0, i))
    return pl.pallas_call(
        context_gradient_body,
        grid_spec=pltpu.PrefetchScalarGridSpec(
            num_scalar_prefetch=1,
            grid=(4,),
            in_specs=[image] * 4 + [low] * 4 + [high] * 4,
            out_specs=[out] * 4,
            scratch_shapes=[pltpu.VMEM((block, half), BF16)],
        ),
        out_shape=[
            jax.ShapeDtypeStruct((seq, rows), kind) for kind in (F32, BF16, F32, BF16)
        ],
        compiler_params=params(),
        cost_estimate=cost(8 * seq * half * rows, 20 * 2**20),
        name="context_gradient",
    )(places, *grads, *lows, *highs)


def weight_gradient_body(c0, c1, c2, c3, d0, d1, d2, d3, out_ref):
    context_t = jnp.concatenate([c[...] for c in (c0, c1, c2, c3)], axis=1)
    part = d0.shape[1] // 2
    for half in range(2):
        cols = slice(half * part, (half + 1) * part)
        grads = jnp.concatenate([d[:, cols] for d in (d0, d1, d2, d3)], axis=0)
        total = dot(context_t, grads, (((1,), (0,)), ((), ())))
        for chip in range(16):
            out_ref[chip, 0, :, cols] = total[chip * 24 : (chip + 1) * 24].astype(BF16)


def weight_gradient(contexts, grads):
    rows, seq = contexts[0].shape
    half = grads[0].shape[1]
    return pl.pallas_call(
        weight_gradient_body,
        grid=(4,),
        in_specs=[pl.BlockSpec((rows // 4, seq), lambda i: (i, 0))] * 4
        + [pl.BlockSpec((seq, half), lambda i: (0, 0))] * 4,
        out_specs=pl.BlockSpec((16, 1, 24, half), lambda i: (0, i, 0, 0)),
        out_shape=jax.ShapeDtypeStruct((16, 4, 24, half), BF16),
        compiler_params=params(),
        cost_estimate=cost(8 * seq * half * rows, 12 * 2**20),
        name="weight_gradient",
    )(*contexts, *grads)


def sums_on_owners(terms, zh, c):
    sums = jnp.sum(terms.astype(F32), axis=0).astype(BF16)
    mine = lax.dynamic_index_in_dim(sums, zh, 0, False).astype(F32)
    for step in (1, 2, 3):
        away = lax.dynamic_index_in_dim(sums, (zh + step) % 4, 0, False)
        mine = mine + lax.ppermute(away, "zh", ring(4, step)).astype(F32)
    mine = mine.reshape(2, 12, -1)
    kept = jnp.where(c == 0, mine[0], mine[1])
    sent = jnp.where(c == 0, mine[1], mine[0])
    return kept, lax.ppermute(sent, "c", SWAP)


def per_device(queries, keys, values, grad_output, weight_codes, weight_scales):
    _, seq, total = queries.shape
    features = grad_output.shape[2]
    q, k, v = (a.reshape(seq, total) for a in (queries, keys, values))
    grad = grad_output.reshape(seq, features)
    zh, zl, xl, c, y = (lax.axis_index(name) for name in ("zh", "zl", "xl", "c", "y"))
    width = 384
    own_parity = zl.astype(jnp.int32).reshape(1)
    other_parity = 1 - own_parity

    piece, sent = restore(weight_codes, weight_scales.T)
    arrived = lax.ppermute(sent, "c", SWAP)
    pair = jnp.where(
        c == 0, jnp.concatenate([piece, arrived], 0), jnp.concatenate([arrived, piece], 0)
    )
    behind = [lax.ppermute(pair, "zh", ring(4, step)) for step in (1, -1)]
    edge = pair.shape[0] // 2
    relayed = [
        lax.ppermute(behind[0][:edge], "zh", ring(4, 1)),
        lax.ppermute(behind[1][edge:], "zh", ring(4, -1)),
    ]
    (late_parity,) = after((other_parity,), (behind[0],))
    context_other = forward(late_parity, q, k, v, width)
    (pair,) = after((pair,), (context_other,))
    low, high = by_zh(pair, behind + relayed)
    beside_low = lax.ppermute(low, ("xl", "xh"), x_ring(1))
    beside_high = lax.ppermute(high, ("xl", "xh"), x_ring(-1))

    half = features // 2
    (late_grad,) = after((grad,), (context_other,))
    mine, other = (
        lax.dynamic_slice_in_dim(late_grad, side * half, half, 1) for side in (c, 1 - c)
    )
    d1 = lax.ppermute(other, "c", SWAP)

    (context_other,) = after((context_other,), tuple(behind))
    c2 = lax.ppermute(context_other, "zl", SWAP)

    low, high = by_xl(low, high, beside_low, beside_high)
    near, diagonal = after((mine, other), (c2, low, d1))
    d2 = lax.ppermute(near, "zl", SWAP)
    d3 = lax.ppermute(diagonal, ("zl", "c"), [(i, 3 - i) for i in range(4)])
    grads = (mine, d1, d2, d3)
    (late_parity,) = after((own_parity,), (low,))
    context_own = forward(late_parity, q, k, v, width)
    lows, highs = ([piece.reshape(-1, width)] for piece in (low, high))
    for step in (1, -1):
        lows.append(lax.ppermute(lows[0], "y", ring(4, step)))
        highs.append(lax.ppermute(highs[0], "y", ring(4, step)))
    lows.append(lax.ppermute(lows[1], "y", ring(4, 1)))
    highs.append(lax.ppermute(highs[2], "y", ring(4, -1)))
    sent_own, sent_away = after((context_own, c2), (*lows[1:3], *highs[1:3]))
    c1 = lax.ppermute(sent_own, "c", SWAP)
    c3 = lax.ppermute(sent_away, "c", SWAP)

    terms = weight_gradient((context_own, c1, c2, c3), grads)
    (terms,) = after((terms,), (*lows[2:], *highs[1:]))
    terms = lax.all_to_all(terms, ("xl", "xh", "y"), 0, 0, tiled=True)

    places = jnp.stack([y, (y + 3) % 4, (y + 1) % 4, (y + 2) % 4]).astype(jnp.int32)
    g0, g1, g2, g3 = context_gradient(places, grads, lows, highs)
    r3 = lax.ppermute(g3, "c", SWAP)
    r1 = lax.ppermute(g1, "c", SWAP)
    g_other = lax.ppermute((g2 + r3.astype(F32)).astype(BF16), "zl", SWAP)
    first = backward(own_parity, q, k, v, (g0, r1), width)
    outs = backward(other_parity, q, k, v, (g_other,), width, first)

    (terms,) = after((terms,), tuple(outs))
    kept, got = sums_on_owners(terms, zh, c)
    grad_weight = jnp.where(
        c == 0, jnp.concatenate([kept, got], 1), jnp.concatenate([got, kept], 1)
    )
    return tuple(out.reshape(1, seq, total) for out in outs) + (grad_weight,)


def solution(mesh):
    split = Mesh(mesh.devices.reshape(4, 2, 2, 2, 2, 4), AXES)
    image = P(AXES, None, None)
    return jax.shard_map(
        per_device,
        mesh=split,
        in_specs=(image, image, image, image, P(SHARD, None), P(SHARD, None)),
        out_specs=(image, image, image, P(AXES, None)),
        check_vma=False,
    )
```
